32 devices in a mesh: groups: 2 (over y), view: 4 (over z), head: 2 (over x), dp: 2 (over core).
Axes of the slice: x: 2, y: 2, z: 4, core: 2. Of those that a mesh axis runs over, the one named last changes fastest.
Arguments:
- ray_tokens: bfloat16 [512, 1024], P(('groups', 'view', 'dp')), parts along dimension 0, may hold values from -6 to 6
- up_weight: bfloat16 [1024, 4096], P('dp', 'head'), may hold values from -0.1875 to 0.1875
- down_weight: bfloat16 [1024, 4096], P('dp', 'head'), may hold values from -0.09375 to 0.09375
- key_weight: bfloat16 [1024, 5120], P('dp', 'head'), may hold values from -0.1875 to 0.1875
- value_weight: bfloat16 [1024, 5120], P('dp', 'head'), may hold values from -0.1875 to 0.1875
- video_queries: bfloat16 [2048, 5120], P(('groups', 'view', 'dp'), 'head'), parts along dimension 0, may hold values from -204 to 204
- video_keys: bfloat16 [2048, 5120], P(('groups', 'view', 'dp'), 'head'), parts along dimension 0, may hold values from -6 to 6
- video_values: bfloat16 [2048, 5120], P(('groups', 'view', 'dp'), 'head'), parts along dimension 0, may hold values from -6 to 6
- cross_queries: bfloat16 [2048, 5120], P(('groups', 'view', 'dp'), 'head'), parts along dimension 0, may hold values from -204 to 204
Outputs:
- attended: bfloat16 [2048, 5120], P(('groups', 'view', 'dp'), 'head'), parts along dimension 0
The draws below stay inside these ranges and needn't reach their ends.
There are 2 independent parts, one for each index of `groups`. The reference program is written for one: setup_inputs(seed, part) draws one part's arguments, and reference() takes and returns one part's arrays. A program takes and returns all parts, laid end to end along the dimension named above; an argument that names none is the same for every part. Nothing has to cross between parts.
All inputs are finite; a program needn't handle non-finite values.
Results may differ from the reference program's by a relative error of at most 0.025.
Values may be sent and summed in bfloat16 or wider, within the bound.
A program may use at most 64 MiB of HBM per device.

```python
import jax
import jax.numpy as jnp
from jax import lax

HEAD_DIM = 128
DR = 1024
FFR = 4096
D = 5120
TOKENS = 1024
RAYS = 256


def query_rows(key, row_count, spread):
    first = jax.random.fold_in(key, 0)
    base = jax.random.normal(first, (row_count, D), jnp.float32) * spread
    return jnp.clip(base, -6.0 * spread, 6.0 * spread).astype(jnp.bfloat16)


def draw_video_queries(key, part):
    return query_rows(jax.random.fold_in(key, 11), TOKENS, 2.0)


def draw_cross_queries(key, part):
    return query_rows(jax.random.fold_in(key, 23), TOKENS, 2.0)


def level_of(stream_key, extent, cuts, smallest, largest):
    level, own = 1.0, jax.random.fold_in(stream_key, 6)
    for dim, shards_of in cuts:
        steps = jnp.exp(jax.random.uniform(jax.random.fold_in(own, dim), (shards_of,), jnp.float32, smallest / len(cuts), largest / len(cuts)))
        level = level * jnp.repeat(steps, extent[dim] // shards_of).reshape([-1 if axis == dim else 1 for axis in range(len(extent))])
    return level


def gaussian(key, dims, width, bound, cuts=(), held_as=jnp.bfloat16):
    entries = width * jax.random.normal(key, dims, jnp.float32)
    if cuts:
        entries = entries * level_of(key, dims, cuts, -0.22, 0.18)
    return jnp.clip(entries, -bound, bound).astype(held_as)


def setup_inputs(seed: int = 0, part: int = 0) -> dict:
    key_of = jax.random.split(jax.random.key(seed), 10)
    part_keys = jax.random.split(jax.random.fold_in(key_of[9], part), 10)
    ray_tokens = gaussian(part_keys[0], (RAYS, DR), 1.0, 6.0, ((0, 8),))
    up_weight = gaussian(key_of[1], (DR, FFR), DR ** -0.5, 0.1875, ((0, 2), (1, 2)))
    down_weight = gaussian(key_of[2], (DR, FFR), FFR ** -0.5, 0.09375, ((0, 2), (1, 2)))
    key_weight = gaussian(key_of[3], (DR, D), DR ** -0.5, 0.1875, ((0, 2), (1, 2)))
    value_weight = gaussian(key_of[4], (DR, D), DR ** -0.5, 0.1875, ((0, 2), (1, 2)))
    video_queries = draw_video_queries(jax.random.fold_in(jax.random.fold_in(key_of[9], part), 71), part)
    video_keys = gaussian(part_keys[6], (TOKENS, D), 1.0, 6.0, ((0, 8), (1, 2)))
    video_values = gaussian(part_keys[7], (TOKENS, D), 1.0, 6.0, ((0, 8), (1, 2)))
    cross_queries = draw_cross_queries(jax.random.fold_in(jax.random.fold_in(key_of[9], part), 71), part)
    return dict(ray_tokens=ray_tokens, up_weight=up_weight, down_weight=down_weight, key_weight=key_weight, value_weight=value_weight, video_queries=video_queries, video_keys=video_keys, video_values=video_values, cross_queries=cross_queries)


epsilon = 1e-06

def rms_normed(values_in):
    widened = values_in.astype(jnp.float32)
    mean_square = lax.optimization_barrier(jnp.mean(widened * widened, axis=1, keepdims=True))
    return widened * lax.rsqrt(mean_square + epsilon)

def attention(queries, keys, value_matrix):
    row_count = queries.shape[0]
    head_count = queries.shape[1] // HEAD_DIM
    query_head_rows = queries.reshape(row_count, head_count, HEAD_DIM).transpose(1, 0, 2)
    key_head_rows = keys.reshape(keys.shape[0], head_count, HEAD_DIM).transpose(1, 0, 2)
    value_head_rows = value_matrix.reshape(value_matrix.shape[0], head_count, HEAD_DIM).transpose(1, 0, 2)

    def per_head(operands):
        query_head, key_head, value_head = operands
        scores = jnp.dot(query_head, key_head.T, preferred_element_type=jnp.float32) * HEAD_DIM ** (-0.5)
        largest_score = lax.optimization_barrier(jnp.max(scores, axis=1, keepdims=True))
        weights = jnp.exp(scores - largest_score)
        row_sums = lax.optimization_barrier(jnp.sum(weights, axis=1, keepdims=True))
        mixed = jnp.dot(weights.astype(jnp.bfloat16), value_head, preferred_element_type=jnp.float32)
        return mixed / row_sums
    result = lax.map(per_head, (query_head_rows, key_head_rows, value_head_rows))
    return result.transpose(1, 0, 2).reshape(row_count, head_count * HEAD_DIM)

def reference(ray_tokens, up_weight, down_weight, key_weight, value_weight, video_queries, video_keys, video_values, cross_queries):
    normed = rms_normed(ray_tokens).astype(jnp.bfloat16)
    hidden = jax.nn.gelu(jnp.dot(normed, up_weight, preferred_element_type=jnp.float32)).astype(jnp.bfloat16)
    branch = jnp.dot(hidden, down_weight.T, preferred_element_type=jnp.float32)
    rays = (ray_tokens.astype(jnp.float32) + branch).astype(jnp.bfloat16)
    ray_keys = jnp.dot(rays, key_weight, preferred_element_type=jnp.float32).astype(jnp.bfloat16)
    ray_values = jnp.dot(rays, value_weight, preferred_element_type=jnp.float32).astype(jnp.bfloat16)
    own = attention(video_queries, video_keys, video_values)
    cross = attention(cross_queries, ray_keys, ray_values)
    return (own + cross).astype(jnp.bfloat16)
```

```python
import functools

import jax
import jax.numpy as jnp
from jax import lax
from jax.experimental import pallas as pl
from jax.experimental.pallas import tpu as pltpu
from jax.sharding import PartitionSpec as P

HEAD_DIM = 128


epsilon = 1e-06


def rms_normed(values_in):
    widened = values_in.astype(jnp.float32)
    mean_square = jnp.mean(widened * widened, axis=1, keepdims=True)
    return widened * lax.rsqrt(mean_square + epsilon)


def empty_state(head_count, row_count):
    running_max = jnp.full((head_count, row_count), -1e30, jnp.float32)
    running_sum = jnp.zeros((head_count, row_count), jnp.float32)
    weighted = jnp.zeros((head_count, row_count, HEAD_DIM), jnp.float32)
    return (running_max, running_sum, weighted)


def absorb(state_now, query_head_rows, key_piece, value_piece):
    running_max, running_sum, weighted = state_now
    head_count = query_head_rows.shape[1]
    key_head_rows = key_piece.reshape(key_piece.shape[0], head_count, HEAD_DIM)
    value_head_rows = value_piece.reshape(value_piece.shape[0], head_count, HEAD_DIM)
    scores = jnp.einsum(
        "xrz,frz->rxf", query_head_rows, key_head_rows, preferred_element_type=jnp.float32
    ) * HEAD_DIM ** (-0.5)
    new_max = jnp.maximum(running_max, jnp.max(scores, axis=2))
    exponent = jnp.exp(scores - new_max[:, :, None])
    running_sum = jnp.sum(exponent, axis=2)
    weighted = jnp.einsum(
        "bau,uby->bay",
        exponent.astype(jnp.bfloat16),
        value_head_rows,
        preferred_element_type=jnp.float32,
    )
    return (new_max, running_sum, weighted)


def finish(state_now):
    running_max, running_sum, weighted = state_now
    result = weighted / running_sum[:, :, None]
    head_count, row_count = running_sum.shape
    return result.transpose(1, 0, 2).reshape(row_count, head_count * HEAD_DIM)


def body(
    ray_tokens,
    up_weight,
    down_weight,
    key_weight,
    value_weight,
    video_queries,
    video_keys,
    video_values,
    cross_queries,
):
    row_count = video_queries.shape[0]
    head_count = video_queries.shape[1] // HEAD_DIM
    up_full, down_full, key_full, value_full = (
        lax.all_gather(up_weight, "dp", axis=0, tiled=True),
        lax.all_gather(down_weight, "dp", axis=0, tiled=True),
        lax.all_gather(key_weight, "dp", axis=0, tiled=True),
        lax.all_gather(value_weight, "dp", axis=0, tiled=True),
    )
    normed = rms_normed(ray_tokens).astype(jnp.bfloat16)
    hidden = jax.nn.gelu(jnp.dot(normed, up_full, preferred_element_type=jnp.float32)).astype(
        jnp.bfloat16
    )
    partial_branch = lax.dot_general(
        hidden, down_full, (((1,), (1,)), ((), ())), preferred_element_type=jnp.float32
    )
    branch = lax.psum(partial_branch, "head")
    rays = (ray_tokens.astype(jnp.float32) + branch).astype(jnp.bfloat16)
    cross_heads = cross_queries.reshape(row_count, head_count, HEAD_DIM)
    piece = lax.all_gather(rays, ("view", "dp"), axis=0, tiled=True)
    piece_keys = jnp.dot(piece, key_full, preferred_element_type=jnp.float32).astype(jnp.bfloat16)
    piece_values = jnp.dot(piece, value_full, preferred_element_type=jnp.float32).astype(
        jnp.bfloat16
    )
    cross_state = absorb(empty_state(head_count, row_count), cross_heads, piece_keys, piece_values)
    cross = finish(cross_state)
    local_head_group = video_queries.reshape(row_count, head_count, HEAD_DIM)
    own_state = absorb(
        empty_state(head_count, row_count),
        local_head_group,
        lax.all_gather(video_keys, ("view", "dp"), axis=0, tiled=True),
        lax.all_gather(video_values, ("view", "dp"), axis=0, tiled=True),
    )
    own = finish(own_state)
    return (own + cross).astype(jnp.bfloat16)


MESH = pl.DeviceIdType.MESH
QUERY_BLOCK = 256
FIRST_HEADS = 2
SECOND_HEADS = 1


def softmax_mix(queries, keys, values):
    scores = lax.dot_general(
        queries, keys, (((1,), (1,)), ((), ())), preferred_element_type=jnp.float32
    )
    largest = jnp.max(scores, axis=1, keepdims=True)
    weights = jnp.exp((scores - largest) * HEAD_DIM ** (-0.5))
    row_sums = jnp.sum(weights, axis=1, keepdims=True)
    mixed = jnp.dot(weights.astype(jnp.bfloat16), values, preferred_element_type=jnp.float32)
    return mixed / row_sums


def columns_of(index):
    return pl.ds(pl.multiple_of(index * HEAD_DIM, HEAD_DIM), HEAD_DIM)


def kernel(
    views,
    head_parts,
    ray_ref,
    up_ref,
    down_ref,
    key_ref,
    value_ref,
    query_ref,
    video_key_ref,
    video_value_ref,
    cross_query_ref,
    own_ref,
    cross_out_ref,
    up_full,
    down_full,
    key_full,
    value_full,
    cross_queries,
    ray_tokens,
    hidden_ref,
    partials_out,
    partials_in,
    rays,
    query_heads,
    pair_heads,
    own_heads,
    cross_ref,
    weight_local,
    weight_send,
    weight_recv,
    query_recv,
    pair_recv,
    relay_recv,
    bulk_send,
    relay_send,
    partial_send,
    partial_recv,
    ray_send,
    ray_recv,
    share_send,
    share_recv,
    pair_ray_send,
    pair_ray_recv,
    own_send,
    own_recv,
    own_local,
    cross_sem,
):
    view = lax.axis_index("view")
    part = lax.axis_index("head")
    core = lax.axis_index("dp")
    other = 1 - core
    rows = query_ref.shape[0]
    head_count = query_ref.shape[1] // HEAD_DIM
    per_view = head_count // views
    ray_rows = ray_ref.shape[0]
    half = up_ref.shape[0]
    inner = up_ref.shape[1]
    share = ray_ref.shape[1] // head_parts
    side = views // 2

    peers = [lax.rem(view + step, views) for step in range(1, views)]
    part_peers = [lax.rem(part + step, head_parts) for step in range(1, head_parts)]

    barrier = pltpu.get_barrier_semaphore()
    pl.semaphore_signal(barrier, inc=1, device_id={"dp": other}, device_id_type=MESH)
    for peer in peers:
        pl.semaphore_signal(barrier, inc=1, device_id={"view": peer}, device_id_type=MESH)
    for peer in part_peers:
        pl.semaphore_signal(barrier, inc=1, device_id={"head": peer}, device_id_type=MESH)

    depth = pl.ds(pl.multiple_of(core * half, half), half)
    weight_pairs = (
        (up_ref, up_full.at[core]),
        (down_ref, down_full.at[core]),
        (key_ref, key_full.at[depth]),
        (value_ref, value_full.at[depth]),
    )
    local_copies = [
        pltpu.make_async_copy(source, slot, weight_local.at[index])
        for index, (source, slot) in enumerate(weight_pairs)
    ]
    local_copies.append(
        pltpu.make_async_copy(cross_query_ref, cross_queries, weight_local.at[4])
    )
    remote_copies = [
        pltpu.make_async_remote_copy(
            src_ref=source,
            dst_ref=slot,
            send_sem=weight_send.at[index],
            recv_sem=weight_recv.at[index],
            device_id={"dp": other},
            device_id_type=MESH,
        )
        for index, (source, slot) in enumerate(weight_pairs)
    ]
    local_copies.append(pltpu.make_async_copy(ray_ref, ray_tokens, weight_local.at[5]))
    for copy in local_copies[::-1]:
        copy.start()

    own_rows = pl.ds(pl.multiple_of(view * rows, rows), rows)

    def keep_heads(index, carry):
        columns = columns_of(view * per_view + index)
        pltpu.make_async_copy(
            query_ref.at[:, columns], query_heads.at[index, own_rows], query_recv.at[index]
        ).start()
        pltpu.make_async_copy(
            video_key_ref.at[:, columns],
            pair_heads.at[index, core, 0, own_rows],
            pair_recv.at[index],
        ).start()
        pltpu.make_async_copy(
            video_value_ref.at[:, columns],
            pair_heads.at[index, core, 1, own_rows],
            pair_recv.at[index],
        ).start()
        return carry

    lax.fori_loop(0, per_view, keep_heads, 0)

    def send_heads(index, carry):
        for peer in peers:
            columns = columns_of(peer * per_view + index)
            for tensor, (source, target, arrived) in enumerate((
                (video_key_ref, pair_heads.at[index, core, 0, own_rows], pair_recv.at[index]),
                (video_value_ref, pair_heads.at[index, core, 1, own_rows], pair_recv.at[index]),
                (query_ref, query_heads.at[index, own_rows], query_recv.at[index]),
            )):
                pltpu.make_async_remote_copy(
                    src_ref=source.at[:, columns],
                    dst_ref=target,
                    send_sem=bulk_send.at[tensor],
                    recv_sem=arrived,
                    device_id={"view": peer},
                    device_id_type=MESH,
                ).start()
        return carry

    first_heads = min(FIRST_HEADS, per_view)
    pl.semaphore_wait(barrier, len(peers) + len(part_peers) + 1)
    for copy in remote_copies[:2]:
        copy.start()
    lax.fori_loop(0, first_heads, send_heads, 0)
    for copy in remote_copies[2:]:
        copy.start()

    local_copies[5].wait()
    tokens = ray_tokens[...]
    normed = rms_normed(tokens).astype(jnp.bfloat16)
    local_copies[0].wait()
    remote_copies[0].wait_recv()
    tile = min(512, inner)

    def up_tile(index, carry):
        columns = pl.ds(pl.multiple_of(index * tile, tile), tile)
        total = jnp.dot(normed[:, :half], up_full[0, :, columns], preferred_element_type=jnp.float32)
        total += jnp.dot(normed[:, half:], up_full[1, :, columns], preferred_element_type=jnp.float32)
        hidden_ref[:, columns] = jax.nn.gelu(total).astype(jnp.bfloat16)
        return carry

    lax.fori_loop(0, inner // tile, up_tile, 0)
    local_copies[1].wait()
    remote_copies[1].wait_recv()
    branch = jnp.concatenate(
        [
            lax.dot_general(
                hidden_ref[...],
                down_full[index],
                (((1,), (1,)), ((), ())),
                preferred_element_type=jnp.float32,
            )
            for index in range(2)
        ],
        axis=1,
    )
    for index in range(head_parts):
        partials_out[index] = branch[:, index * share : (index + 1) * share]
    partial_copies = [
        pltpu.make_async_remote_copy(
            src_ref=partials_out.at[peer],
            dst_ref=partials_in.at[step],
            send_sem=partial_send.at[step],
            recv_sem=partial_recv.at[step],
            device_id={"head": peer},
            device_id_type=MESH,
        )
        for step, peer in enumerate(part_peers)
    ]
    for copy in partial_copies:
        copy.start()
    for copy in partial_copies:
        copy.wait_recv()
    total_share = partials_out[part]
    for index in range(head_parts - 1):
        total_share += partials_in[index]
    share_columns = pl.ds(pl.multiple_of(part * share, share), share)
    rays[core, part, view] = (
        ray_tokens[:, share_columns].astype(jnp.float32) + total_share
    ).astype(jnp.bfloat16)
    side_start = (view // side) * side
    far_start = side - side_start
    gate = jnp.where(side_start == 0, side - 1, side)
    far_gate = 2 * side - 1 - gate
    side_peers = [side_start + lax.rem(view - side_start + step, side) for step in range(1, side)]

    def ray_copy(source, peer, index, arrived):
        return pltpu.make_async_remote_copy(
            src_ref=source,
            dst_ref=source,
            send_sem=ray_send.at[index],
            recv_sem=ray_recv.at[arrived],
            device_id={"view": peer},
            device_id_type=MESH,
        )

    mine = rays.at[core, part, view]
    far_slots = rays.at[core, part, pl.ds(far_start, side)]
    ray_copies = [ray_copy(mine, peer, step, step) for step, peer in enumerate(side_peers)]
    far_copy = ray_copy(mine, far_gate, side - 1, side - 1)
    far_copy.start()
    for copy in ray_copies:
        copy.start()
    second_heads = min(first_heads + SECOND_HEADS, per_view)
    lax.fori_loop(first_heads, second_heads, send_heads, 0)

    def relay(index):
        return pltpu.make_async_remote_copy(
            src_ref=pair_heads.at[index, core],
            dst_ref=pair_heads.at[index, core],
            send_sem=relay_send.at[index],
            recv_sem=relay_recv.at[index],
            device_id={"dp": other},
            device_id_type=MESH,
        )

    def pass_on(index, carry):
        arrived = pair_heads.at[index, core]
        pltpu.make_async_copy(arrived, arrived, pair_recv.at[index]).wait()
        relay(index).start()
        return carry

    def attend(index, carry):
        arrived = query_heads.at[index]
        pltpu.make_async_copy(arrived, arrived, query_recv.at[index]).wait()
        relay(index).wait_recv()
        keys = pair_heads[index, :, 0].reshape(2 * views * rows, HEAD_DIM)
        values = pair_heads[index, :, 1].reshape(2 * views * rows, HEAD_DIM)
        block = min(QUERY_BLOCK, views * rows)

        def attend_block(piece, inner_carry):
            span = pl.ds(pl.multiple_of(piece * block, block), block)
            own_heads[index, span] = softmax_mix(query_heads[index, span], keys, values).astype(
                jnp.bfloat16
            )
            return inner_carry

        lax.fori_loop(0, views * rows // block, attend_block, 0)
        columns = columns_of(view * per_view + index)
        pltpu.make_async_copy(
            own_heads.at[index, own_rows], own_ref.at[:, columns], own_local
        ).start()
        for peer in peers:
            pltpu.make_async_remote_copy(
                src_ref=own_heads.at[index, pl.ds(pl.multiple_of(peer * rows, rows), rows)],
                dst_ref=own_ref.at[:, columns],
                send_sem=own_send,
                recv_sem=own_recv,
                device_id={"view": peer},
                device_id_type=MESH,
            ).start()
        return carry

    lax.fori_loop(0, first_heads, pass_on, 0)
    pltpu.make_async_copy(far_slots, far_slots, ray_recv.at[side - 1]).wait()
    gate_copies = [
        ray_copy(far_slots, peer, side + step, side - 1) for step, peer in enumerate(side_peers)
    ]

    @pl.when(view == gate)
    def _():
        for copy in gate_copies:
            copy.start()

    lax.fori_loop(second_heads, per_view, send_heads, 0)
    for copy in ray_copies:
        copy.wait_recv()
    share_copies = [
        pltpu.make_async_remote_copy(
            src_ref=rays.at[core, part],
            dst_ref=rays.at[core, part],
            send_sem=share_send.at[step],
            recv_sem=share_recv.at[step],
            device_id={"head": peer},
            device_id_type=MESH,
        )
        for step, peer in enumerate(part_peers)
    ]
    for copy in share_copies:
        copy.start()
    lax.fori_loop(0, first_heads, attend, 0)
    lax.fori_loop(first_heads, second_heads, pass_on, 0)
    for copy in share_copies:
        copy.wait_recv()
    ray_relay = pltpu.make_async_remote_copy(
        src_ref=rays.at[core],
        dst_ref=rays.at[core],
        send_sem=pair_ray_send,
        recv_sem=pair_ray_recv,
        device_id={"dp": other},
        device_id_type=MESH,
    )
    ray_relay.start()
    lax.fori_loop(first_heads, second_heads, attend, 0)

    ray_relay.wait_recv()
    for index in (2, 3):
        local_copies[index].wait()
        remote_copies[index].wait_recv()
    local_copies[4].wait()
    ray_shares = [
        rays[:, index].reshape(2 * views * ray_rows, share) for index in range(head_parts)
    ]
    group = 2 if head_count % 2 == 0 else 1
    width = group * HEAD_DIM

    def cross_group(index, carry):
        columns = pl.ds(pl.multiple_of(index * width, width), width)

        def project(full):
            total = 0.0
            for index, ray_share in enumerate(ray_shares):
                total += jnp.dot(
                    ray_share,
                    full[index * share : (index + 1) * share, columns],
                    preferred_element_type=jnp.float32,
                )
            return total.astype(jnp.bfloat16)

        keys, values = project(key_full), project(value_full)
        queries = cross_queries[:, columns]
        results = []
        for lane in range(group):
            span = slice(lane * HEAD_DIM, (lane + 1) * HEAD_DIM)
            results.append(softmax_mix(queries[:, span], keys[:, span], values[:, span]))
        cross_ref[:, columns] = jnp.concatenate(results, axis=1)
        return carry

    lax.fori_loop(0, head_count // group, cross_group, 0)
    cross_copy = pltpu.make_async_copy(cross_ref, cross_out_ref, cross_sem)
    cross_copy.start()

    lax.fori_loop(second_heads, per_view, pass_on, 0)
    lax.fori_loop(second_heads, per_view, attend, 0)

    sent_copies = remote_copies + partial_copies + ray_copies + share_copies
    for copy in sent_copies + [far_copy, ray_relay]:
        copy.wait_send()

    @pl.when(view == gate)
    def _():
        for copy in gate_copies:
            copy.wait_send()

    def relay_sent(index, carry):
        relay(index).wait_send()
        return carry

    lax.fori_loop(0, per_view, relay_sent, 0)
    for tensor in range(3):
        sent = query_heads.at[:, pl.ds(0, (views - 1) * rows)]
        pltpu.make_async_copy(sent, sent, bulk_send.at[tensor]).wait()
    cross_copy.wait()
    kept = own_heads.at[:, pl.ds(0, rows)]
    pltpu.make_async_copy(kept, kept, own_local).wait()
    returned = own_heads.at[:, pl.ds(0, (views - 1) * rows)]
    pltpu.make_async_copy(returned, returned, own_send).wait()
    pltpu.make_async_copy(returned, returned, own_recv).wait()


def fused_body(views, head_parts, *args):
    ray_tokens, up_weight, down_weight, key_weight, value_weight, video_queries = args[:6]
    rows, columns = video_queries.shape
    per_view = columns // HEAD_DIM // views
    ray_rows, ray_width = ray_tokens.shape
    half, inner = up_weight.shape
    share = ray_width // head_parts
    bf16, f32 = jnp.bfloat16, jnp.float32
    dma = pltpu.SemaphoreType.DMA
    anywhere = pl.BlockSpec(memory_space=pl.ANY)
    args = [pltpu.with_memory_space_constraint(arg, pltpu.HBM) for arg in args]
    own, cross = pl.pallas_call(
        functools.partial(kernel, views, head_parts),
        out_shape=(pltpu.VMEM((rows, columns), bf16), pltpu.VMEM((rows, columns), f32)),
        in_specs=[anywhere] * 9,
        out_specs=(anywhere, anywhere),
        scratch_shapes=[
            pltpu.VMEM((2,) + up_weight.shape, bf16),
            pltpu.VMEM((2,) + down_weight.shape, bf16),
            pltpu.VMEM((2 * half, columns), bf16),
            pltpu.VMEM((2 * half, columns), bf16),
            pltpu.VMEM((rows, columns), bf16),
            pltpu.VMEM((ray_rows, ray_width), bf16),
            pltpu.VMEM((ray_rows, inner), bf16),
            pltpu.VMEM((head_parts, ray_rows, share), f32),
            pltpu.VMEM((head_parts, ray_rows, share), f32),
            pltpu.VMEM((2, head_parts, views, ray_rows, share), bf16),
            pltpu.VMEM((per_view, views * rows, HEAD_DIM), bf16),
            pltpu.VMEM((per_view, 2, 2, views * rows, HEAD_DIM), bf16),
            pltpu.VMEM((per_view, views * rows, HEAD_DIM), bf16),
            pltpu.VMEM((rows, columns), f32),
            dma((6,)),
            dma((4,)),
            dma((4,)),
            dma((per_view,)),
            dma((per_view,)),
            dma((per_view,)),
            dma((3,)),
            dma((per_view,)),
            dma((max(head_parts - 1, 1),)),
            dma((max(head_parts - 1, 1),)),
            dma((views,)),
            dma((views,)),
            dma((max(head_parts - 1, 1),)),
            dma((max(head_parts - 1, 1),)),
            dma,
            dma,
            dma,
            dma,
            dma,
            dma,
        ],
        compiler_params=pltpu.CompilerParams(
            collective_id=0, has_side_effects=True, vmem_limit_bytes=48 * 2**20
        ),
    )(*args)
    return (cross + own.astype(f32)).astype(bf16)


def solution(mesh):
    views, head_parts = mesh.shape["view"], mesh.shape["head"]

    def routed(*args):
        head_count = args[5].shape[1] // HEAD_DIM
        if (
            mesh.shape["dp"] == 2
            and views % 2 == 0
            and head_count % views == 0
            and args[0].shape[1] % (head_parts * HEAD_DIM) == 0
        ):
            return fused_body(views, head_parts, *args)
        return body(*args)

    in_specs = (
        P(("groups", "view", "dp"), None),
        P("dp", "head"),
        P("dp", "head"),
        P("dp", "head"),
        P("dp", "head"),
        P(("groups", "view", "dp"), "head"),
        P(("groups", "view", "dp"), "head"),
        P(("groups", "view", "dp"), "head"),
        P(("groups", "view", "dp"), "head"),
    )
    out_specs = P(("groups", "view", "dp"), "head")
    return jax.shard_map(routed, mesh=mesh, in_specs=in_specs, out_specs=out_specs, check_vma=False)
```

```python
import functools

import jax
import jax.numpy as jnp
from jax import lax
from jax.experimental import pallas as pl
from jax.experimental.pallas import tpu as pltpu
from jax.sharding import PartitionSpec as P

HEAD_DIM = 128


epsilon = 1e-06


def rms_normed(values_in):
    widened = values_in.astype(jnp.float32)
    mean_square = jnp.mean(widened * widened, axis=1, keepdims=True)
    return widened * lax.rsqrt(mean_square + epsilon)


def empty_state(head_count, row_count):
    running_max = jnp.full((head_count, row_count), -1e30, jnp.float32)
    running_sum = jnp.zeros((head_count, row_count), jnp.float32)
    weighted = jnp.zeros((head_count, row_count, HEAD_DIM), jnp.float32)
    return (running_max, running_sum, weighted)


def absorb(state_now, query_head_rows, key_piece, value_piece):
    running_max, running_sum, weighted = state_now
    head_count = query_head_rows.shape[1]
    key_head_rows = key_piece.reshape(key_piece.shape[0], head_count, HEAD_DIM)
    value_head_rows = value_piece.reshape(value_piece.shape[0], head_count, HEAD_DIM)
    scores = jnp.einsum(
        "xrz,frz->rxf", query_head_rows, key_head_rows, preferred_element_type=jnp.float32
    ) * HEAD_DIM ** (-0.5)
    new_max = jnp.maximum(running_max, jnp.max(scores, axis=2))
    exponent = jnp.exp(scores - new_max[:, :, None])
    running_sum = jnp.sum(exponent, axis=2)
    weighted = jnp.einsum(
        "bau,uby->bay",
        exponent.astype(jnp.bfloat16),
        value_head_rows,
        preferred_element_type=jnp.float32,
    )
    return (new_max, running_sum, weighted)


def finish(state_now):
    running_max, running_sum, weighted = state_now
    result = weighted / running_sum[:, :, None]
    head_count, row_count = running_sum.shape
    return result.transpose(1, 0, 2).reshape(row_count, head_count * HEAD_DIM)


def body(
    ray_tokens,
    up_weight,
    down_weight,
    key_weight,
    value_weight,
    video_queries,
    video_keys,
    video_values,
    cross_queries,
):
    row_count = video_queries.shape[0]
    head_count = video_queries.shape[1] // HEAD_DIM
    up_full, down_full, key_full, value_full = (
        lax.all_gather(up_weight, "dp", axis=0, tiled=True),
        lax.all_gather(down_weight, "dp", axis=0, tiled=True),
        lax.all_gather(key_weight, "dp", axis=0, tiled=True),
        lax.all_gather(value_weight, "dp", axis=0, tiled=True),
    )
    normed = rms_normed(ray_tokens).astype(jnp.bfloat16)
    hidden = jax.nn.gelu(jnp.dot(normed, up_full, preferred_element_type=jnp.float32)).astype(
        jnp.bfloat16
    )
    partial_branch = lax.dot_general(
        hidden, down_full, (((1,), (1,)), ((), ())), preferred_element_type=jnp.float32
    )
    branch = lax.psum(partial_branch, "head")
    rays = (ray_tokens.astype(jnp.float32) + branch).astype(jnp.bfloat16)
    cross_heads = cross_queries.reshape(row_count, head_count, HEAD_DIM)
    piece = lax.all_gather(rays, ("view", "dp"), axis=0, tiled=True)
    piece_keys = jnp.dot(piece, key_full, preferred_element_type=jnp.float32).astype(jnp.bfloat16)
    piece_values = jnp.dot(piece, value_full, preferred_element_type=jnp.float32).astype(
        jnp.bfloat16
    )
    cross_state = absorb(empty_state(head_count, row_count), cross_heads, piece_keys, piece_values)
    cross = finish(cross_state)
    local_head_group = video_queries.reshape(row_count, head_count, HEAD_DIM)
    own_state = absorb(
        empty_state(head_count, row_count),
        local_head_group,
        lax.all_gather(video_keys, ("view", "dp"), axis=0, tiled=True),
        lax.all_gather(video_values, ("view", "dp"), axis=0, tiled=True),
    )
    own = finish(own_state)
    return (own + cross).astype(jnp.bfloat16)


MESH = pl.DeviceIdType.MESH
QUERY_BLOCK = 256
FIRST_HEADS = 2
SECOND_HEADS = 1


def softmax_mix(queries, keys, values):
    scores = lax.dot_general(
        queries, keys, (((1,), (1,)), ((), ())), preferred_element_type=jnp.float32
    )
    largest = jnp.max(scores, axis=1, keepdims=True)
    weights = jnp.exp((scores - largest) * HEAD_DIM ** (-0.5))
    row_sums = jnp.sum(weights, axis=1, keepdims=True)
    mixed = jnp.dot(weights.astype(jnp.bfloat16), values, preferred_element_type=jnp.float32)
    return mixed / row_sums


def columns_of(index):
    return pl.ds(pl.multiple_of(index * HEAD_DIM, HEAD_DIM), HEAD_DIM)


def kernel(
    views,
    head_parts,
    ray_ref,
    up_ref,
    down_ref,
    key_ref,
    value_ref,
    query_ref,
    video_key_ref,
    video_value_ref,
    cross_query_ref,
    own_ref,
    cross_out_ref,
    up_full,
    down_full,
    key_full,
    value_full,
    cross_queries,
    ray_tokens,
    hidden_ref,
    partials_out,
    partials_in,
    rays,
    query_heads,
    pair_heads,
    own_heads,
    cross_ref,
    weight_local,
    weight_send,
    weight_recv,
    query_recv,
    pair_recv,
    relay_recv,
    bulk_send,
    relay_send,
    partial_send,
    partial_recv,
    ray_send,
    ray_recv,
    share_send,
    share_recv,
    pair_ray_send,
    pair_ray_recv,
    own_send,
    own_recv,
    own_local,
    cross_sem,
    view_greeted,
    part_greeted,
    core_greeted,
):
    view = lax.axis_index("view")
    part = lax.axis_index("head")
    core = lax.axis_index("dp")
    other = 1 - core
    rows = query_ref.shape[0]
    head_count = query_ref.shape[1] // HEAD_DIM
    per_view = head_count // views
    ray_rows = ray_ref.shape[0]
    half = up_ref.shape[0]
    inner = up_ref.shape[1]
    share = ray_ref.shape[1] // head_parts
    side = views // 2

    peers = [lax.rem(view + step, views) for step in range(1, views)]
    part_peers = [lax.rem(part + step, head_parts) for step in range(1, head_parts)]

    ordered_peers = [jnp.where(step < view, view - 1 - step, step + 1) for step in range(views - 1)]

    barrier = pltpu.get_barrier_semaphore()

    def enter(axis, peer, position):
        @pl.when(peer > position)
        def _():
            pl.semaphore_signal(barrier, inc=1, device_id={axis: peer}, device_id_type=MESH)

    def answer(axis, peer, position, greeted):
        @pl.when(peer < position)
        def _():
            pl.semaphore_signal(
                greeted.at[position], inc=1, device_id={axis: peer}, device_id_type=MESH
            )

    for peer in ordered_peers:
        enter("view", peer, view)
    for peer in part_peers:
        enter("head", peer, part)
    enter("dp", other, core)
    earlier = view + part + core

    @pl.when(earlier > 0)
    def _():
        pl.semaphore_wait(barrier, earlier)

    for peer in ordered_peers:
        answer("view", peer, view, view_greeted)
    for peer in part_peers:
        answer("head", peer, part, part_greeted)
    answer("dp", other, core, core_greeted)

    depth = pl.ds(pl.multiple_of(core * half, half), half)
    weight_pairs = (
        (up_ref, up_full.at[core]),
        (down_ref, down_full.at[core]),
        (key_ref, key_full.at[depth]),
        (value_ref, value_full.at[depth]),
    )
    local_copies = [
        pltpu.make_async_copy(source, slot, weight_local.at[index])
        for index, (source, slot) in enumerate(weight_pairs)
    ]
    local_copies.append(
        pltpu.make_async_copy(cross_query_ref, cross_queries, weight_local.at[4])
    )
    remote_copies = [
        pltpu.make_async_remote_copy(
            src_ref=source,
            dst_ref=slot,
            send_sem=weight_send.at[index],
            recv_sem=weight_recv.at[index],
            device_id={"dp": other},
            device_id_type=MESH,
        )
        for index, (source, slot) in enumerate(weight_pairs)
    ]
    local_copies.append(pltpu.make_async_copy(ray_ref, ray_tokens, weight_local.at[5]))
    own_rows = pl.ds(pl.multiple_of(view * rows, rows), rows)

    def keep_heads(index, carry):
        columns = columns_of(view * per_view + index)
        pltpu.make_async_copy(
            query_ref.at[:, columns], query_heads.at[index, own_rows], query_recv.at[index]
        ).start()
        pltpu.make_async_copy(
            video_key_ref.at[:, columns],
            pair_heads.at[index, core, 0, own_rows],
            pair_recv.at[index],
        ).start()
        pltpu.make_async_copy(
            video_value_ref.at[:, columns],
            pair_heads.at[index, core, 1, own_rows],
            pair_recv.at[index],
        ).start()
        return carry


    def send_head(index, peer):
        columns = columns_of(peer * per_view + index)
        for tensor, (source, target, arrived) in enumerate((
            (video_key_ref, pair_heads.at[index, core, 0, own_rows], pair_recv.at[index]),
            (video_value_ref, pair_heads.at[index, core, 1, own_rows], pair_recv.at[index]),
            (query_ref, query_heads.at[index, own_rows], query_recv.at[index]),
        )):
            pltpu.make_async_remote_copy(
                src_ref=source.at[:, columns],
                dst_ref=target,
                send_sem=bulk_send.at[tensor],
                recv_sem=arrived,
                device_id={"view": peer},
                device_id_type=MESH,
            ).start()

    def send_heads(index, carry):
        for peer in peers:
            send_head(index, peer)
        return carry

    first_heads = min(FIRST_HEADS, per_view)
    for step, peer in enumerate(ordered_peers):
        @pl.when(step >= view)
        def _():
            pl.semaphore_wait(view_greeted.at[step + 1], 1)

        def send_first(index, carry):
            send_head(index, peer)
            return carry

        lax.fori_loop(0, first_heads, send_first, 0)

    @pl.when(core == 0)
    def _():
        pl.semaphore_wait(core_greeted.at[1], 1)

    for copy in remote_copies[:2]:
        copy.start()
    for copy in local_copies[::-1]:
        copy.start()
    lax.fori_loop(0, per_view, keep_heads, 0)
    for copy in remote_copies[2:]:
        copy.start()

    local_copies[5].wait()
    tokens = ray_tokens[...]
    normed = rms_normed(tokens).astype(jnp.bfloat16)
    local_copies[0].wait()
    remote_copies[0].wait_recv()
    tile = min(512, inner)

    def up_tile(index, carry):
        columns = pl.ds(pl.multiple_of(index * tile, tile), tile)
        total = jnp.dot(normed[:, :half], up_full[0, :, columns], preferred_element_type=jnp.float32)
        total += jnp.dot(normed[:, half:], up_full[1, :, columns], preferred_element_type=jnp.float32)
        hidden_ref[:, columns] = jax.nn.gelu(total).astype(jnp.bfloat16)
        return carry

    lax.fori_loop(0, inner // tile, up_tile, 0)
    local_copies[1].wait()
    remote_copies[1].wait_recv()
    branch = jnp.concatenate(
        [
            lax.dot_general(
                hidden_ref[...],
                down_full[index],
                (((1,), (1,)), ((), ())),
                preferred_element_type=jnp.float32,
            )
            for index in range(2)
        ],
        axis=1,
    )
    for index in range(head_parts):
        partials_out[index] = branch[:, index * share : (index + 1) * share]
    partial_copies = [
        pltpu.make_async_remote_copy(
            src_ref=partials_out.at[peer],
            dst_ref=partials_in.at[step],
            send_sem=partial_send.at[step],
            recv_sem=partial_recv.at[step],
            device_id={"head": peer},
            device_id_type=MESH,
        )
        for step, peer in enumerate(part_peers)
    ]
    for later in range(1, head_parts):
        @pl.when(part < later)
        def _():
            pl.semaphore_wait(part_greeted.at[later], 1)

    for copy in partial_copies:
        copy.start()
    for copy in partial_copies:
        copy.wait_recv()
    total_share = partials_out[part]
    for index in range(head_parts - 1):
        total_share += partials_in[index]
    share_columns = pl.ds(pl.multiple_of(part * share, share), share)
    rays[core, part, view] = (
        ray_tokens[:, share_columns].astype(jnp.float32) + total_share
    ).astype(jnp.bfloat16)
    side_start = (view // side) * side
    far_start = side - side_start
    gate = jnp.where(side_start == 0, side - 1, side)
    far_gate = 2 * side - 1 - gate
    side_peers = [side_start + lax.rem(view - side_start + step, side) for step in range(1, side)]

    def ray_copy(source, peer, index, arrived):
        return pltpu.make_async_remote_copy(
            src_ref=source,
            dst_ref=source,
            send_sem=ray_send.at[index],
            recv_sem=ray_recv.at[arrived],
            device_id={"view": peer},
            device_id_type=MESH,
        )

    mine = rays.at[core, part, view]
    far_slots = rays.at[core, part, pl.ds(far_start, side)]
    ray_copies = [ray_copy(mine, peer, step, step) for step, peer in enumerate(side_peers)]
    far_copy = ray_copy(mine, far_gate, side - 1, side - 1)
    far_copy.start()
    for copy in ray_copies:
        copy.start()
    second_heads = min(first_heads + SECOND_HEADS, per_view)
    lax.fori_loop(first_heads, second_heads, send_heads, 0)

    def relay(index):
        return pltpu.make_async_remote_copy(
            src_ref=pair_heads.at[index, core],
            dst_ref=pair_heads.at[index, core],
            send_sem=relay_send.at[index],
            recv_sem=relay_recv.at[index],
            device_id={"dp": other},
            device_id_type=MESH,
        )

    def pass_on(index, carry):
        arrived = pair_heads.at[index, core]
        pltpu.make_async_copy(arrived, arrived, pair_recv.at[index]).wait()
        relay(index).start()
        return carry

    last_view = far_start + side - 1

    def own_copy(index, peer):
        return pltpu.make_async_remote_copy(
            src_ref=own_heads.at[index, pl.ds(pl.multiple_of(peer * rows, rows), rows)],
            dst_ref=own_ref.at[:, columns_of(view * per_view + index)],
            send_sem=own_send,
            recv_sem=own_recv,
            device_id={"view": peer},
            device_id_type=MESH,
        )

    def send_last(index, carry):
        own_copy(index, last_view).start()
        return carry

    def attend(index, carry):
        arrived = query_heads.at[index]
        pltpu.make_async_copy(arrived, arrived, query_recv.at[index]).wait()
        relay(index).wait_recv()
        keys = pair_heads[index, :, 0].reshape(2 * views * rows, HEAD_DIM)
        values = pair_heads[index, :, 1].reshape(2 * views * rows, HEAD_DIM)
        block = min(QUERY_BLOCK, views * rows)

        def attend_block(piece, inner_carry):
            span = pl.ds(pl.multiple_of(piece * block, block), block)
            own_heads[index, span] = softmax_mix(query_heads[index, span], keys, values).astype(
                jnp.bfloat16
            )
            return inner_carry

        lax.fori_loop(0, views * rows // block, attend_block, 0)
        columns = columns_of(view * per_view + index)
        pltpu.make_async_copy(
            own_heads.at[index, own_rows], own_ref.at[:, columns], own_local
        ).start()
        for peer in peers:
            @pl.when(jnp.logical_or(index < 2, peer != last_view))
            def _():
                own_copy(index, peer).start()

        return carry

    lax.fori_loop(0, first_heads, pass_on, 0)
    pltpu.make_async_copy(far_slots, far_slots, ray_recv.at[side - 1]).wait()
    gate_copies = [
        ray_copy(far_slots, peer, side + step, side - 1) for step, peer in enumerate(side_peers)
    ]

    @pl.when(view == gate)
    def _():
        for copy in gate_copies:
            copy.start()

    lax.fori_loop(second_heads, per_view, send_heads, 0)
    for copy in ray_copies:
        copy.wait_recv()
    share_copies = [
        pltpu.make_async_remote_copy(
            src_ref=rays.at[core, part],
            dst_ref=rays.at[core, part],
            send_sem=share_send.at[step],
            recv_sem=share_recv.at[step],
            device_id={"head": peer},
            device_id_type=MESH,
        )
        for step, peer in enumerate(part_peers)
    ]
    for copy in share_copies:
        copy.start()
    lax.fori_loop(0, first_heads, attend, 0)
    lax.fori_loop(first_heads, second_heads, pass_on, 0)
    for copy in share_copies:
        copy.wait_recv()
    ray_relay = pltpu.make_async_remote_copy(
        src_ref=rays.at[core],
        dst_ref=rays.at[core],
        send_sem=pair_ray_send,
        recv_sem=pair_ray_recv,
        device_id={"dp": other},
        device_id_type=MESH,
    )
    ray_relay.start()
    lax.fori_loop(first_heads, second_heads, attend, 0)

    ray_relay.wait_recv()
    for index in (2, 3):
        local_copies[index].wait()
        remote_copies[index].wait_recv()
    local_copies[4].wait()
    ray_shares = [
        rays[:, index].reshape(2 * views * ray_rows, share) for index in range(head_parts)
    ]
    group = 2 if head_count % 2 == 0 else 1
    width = group * HEAD_DIM

    def cross_group(index, carry):
        columns = pl.ds(pl.multiple_of(index * width, width), width)

        def project(full):
            total = 0.0
            for index, ray_share in enumerate(ray_shares):
                total += jnp.dot(
                    ray_share,
                    full[index * share : (index + 1) * share, columns],
                    preferred_element_type=jnp.float32,
                )
            return total.astype(jnp.bfloat16)

        keys, values = project(key_full), project(value_full)
        queries = cross_queries[:, columns]
        results = []
        for lane in range(group):
            span = slice(lane * HEAD_DIM, (lane + 1) * HEAD_DIM)
            results.append(softmax_mix(queries[:, span], keys[:, span], values[:, span]))
        cross_ref[:, columns] = jnp.concatenate(results, axis=1)
        return carry

    lax.fori_loop(0, head_count // group, cross_group, 0)
    cross_copy = pltpu.make_async_copy(cross_ref, cross_out_ref, cross_sem)
    cross_copy.start()

    lax.fori_loop(second_heads, per_view, pass_on, 0)
    lax.fori_loop(second_heads, per_view, attend, 0)
    lax.fori_loop(2, per_view, send_last, 0)

    sent_copies = remote_copies + partial_copies + ray_copies + share_copies
    for copy in sent_copies + [far_copy, ray_relay]:
        copy.wait_send()

    @pl.when(view == gate)
    def _():
        for copy in gate_copies:
            copy.wait_send()

    def relay_sent(index, carry):
        relay(index).wait_send()
        return carry

    lax.fori_loop(0, per_view, relay_sent, 0)
    for tensor in range(3):
        sent = query_heads.at[:, pl.ds(0, (views - 1) * rows)]
        pltpu.make_async_copy(sent, sent, bulk_send.at[tensor]).wait()
    cross_copy.wait()
    kept = own_heads.at[:, pl.ds(0, rows)]
    pltpu.make_async_copy(kept, kept, own_local).wait()
    returned = own_heads.at[:, pl.ds(0, (views - 1) * rows)]
    pltpu.make_async_copy(returned, returned, own_send).wait()
    pltpu.make_async_copy(returned, returned, own_recv).wait()


def fused_body(views, head_parts, *args):
    ray_tokens, up_weight, down_weight, key_weight, value_weight, video_queries = args[:6]
    rows, columns = video_queries.shape
    per_view = columns // HEAD_DIM // views
    ray_rows, ray_width = ray_tokens.shape
    half, inner = up_weight.shape
    share = ray_width // head_parts
    bf16, f32 = jnp.bfloat16, jnp.float32
    dma = pltpu.SemaphoreType.DMA
    anywhere = pl.BlockSpec(memory_space=pl.ANY)
    args = [pltpu.with_memory_space_constraint(arg, pltpu.HBM) for arg in args]
    own, cross = pl.pallas_call(
        functools.partial(kernel, views, head_parts),
        out_shape=(pltpu.VMEM((rows, columns), bf16), pltpu.VMEM((rows, columns), f32)),
        in_specs=[anywhere] * 9,
        out_specs=(anywhere, anywhere),
        scratch_shapes=[
            pltpu.VMEM((2,) + up_weight.shape, bf16),
            pltpu.VMEM((2,) + down_weight.shape, bf16),
            pltpu.VMEM((2 * half, columns), bf16),
            pltpu.VMEM((2 * half, columns), bf16),
            pltpu.VMEM((rows, columns), bf16),
            pltpu.VMEM((ray_rows, ray_width), bf16),
            pltpu.VMEM((ray_rows, inner), bf16),
            pltpu.VMEM((head_parts, ray_rows, share), f32),
            pltpu.VMEM((head_parts, ray_rows, share), f32),
            pltpu.VMEM((2, head_parts, views, ray_rows, share), bf16),
            pltpu.VMEM((per_view, views * rows, HEAD_DIM), bf16),
            pltpu.VMEM((per_view, 2, 2, views * rows, HEAD_DIM), bf16),
            pltpu.VMEM((per_view, views * rows, HEAD_DIM), bf16),
            pltpu.VMEM((rows, columns), f32),
            dma((6,)),
            dma((4,)),
            dma((4,)),
            dma((per_view,)),
            dma((per_view,)),
            dma((per_view,)),
            dma((3,)),
            dma((per_view,)),
            dma((max(head_parts - 1, 1),)),
            dma((max(head_parts - 1, 1),)),
            dma((views,)),
            dma((views,)),
            dma((max(head_parts - 1, 1),)),
            dma((max(head_parts - 1, 1),)),
            dma,
            dma,
            dma,
            dma,
            dma,
            dma,
            pltpu.SemaphoreType.REGULAR((views,)),
            pltpu.SemaphoreType.REGULAR((head_parts,)),
            pltpu.SemaphoreType.REGULAR((2,)),
        ],
        compiler_params=pltpu.CompilerParams(
            collective_id=0, has_side_effects=True, vmem_limit_bytes=48 * 2**20
        ),
    )(*args)
    return (cross + own.astype(f32)).astype(bf16)


def solution(mesh):
    views, head_parts = mesh.shape["view"], mesh.shape["head"]

    def routed(*args):
        head_count = args[5].shape[1] // HEAD_DIM
        if (
            mesh.shape["dp"] == 2
            and views % 2 == 0
            and head_count % views == 0
            and args[0].shape[1] % (head_parts * HEAD_DIM) == 0
        ):
            return fused_body(views, head_parts, *args)
        return body(*args)

    in_specs = (
        P(("groups", "view", "dp"), None),
        P("dp", "head"),
        P("dp", "head"),
        P("dp", "head"),
        P("dp", "head"),
        P(("groups", "view", "dp"), "head"),
        P(("groups", "view", "dp"), "head"),
        P(("groups", "view", "dp"), "head"),
        P(("groups", "view", "dp"), "head"),
    )
    out_specs = P(("groups", "view", "dp"), "head")
    return jax.shard_map(routed, mesh=mesh, in_specs=in_specs, out_specs=out_specs, check_vma=False)
```

```python
import functools

import jax
import jax.numpy as jnp
from jax import lax
from jax.experimental import pallas as pl
from jax.experimental.pallas import tpu as pltpu
from jax.sharding import PartitionSpec as P

HEAD_DIM = 128


epsilon = 1e-06


def rms_normed(values_in):
    widened = values_in.astype(jnp.float32)
    mean_square = jnp.mean(widened * widened, axis=1, keepdims=True)
    return widened * lax.rsqrt(mean_square + epsilon)


def empty_state(head_count, row_count):
    running_max = jnp.full((head_count, row_count), -1e30, jnp.float32)
    running_sum = jnp.zeros((head_count, row_count), jnp.float32)
    weighted = jnp.zeros((head_count, row_count, HEAD_DIM), jnp.float32)
    return (running_max, running_sum, weighted)


def absorb(state_now, query_head_rows, key_piece, value_piece):
    running_max, running_sum, weighted = state_now
    head_count = query_head_rows.shape[1]
    key_head_rows = key_piece.reshape(key_piece.shape[0], head_count, HEAD_DIM)
    value_head_rows = value_piece.reshape(value_piece.shape[0], head_count, HEAD_DIM)
    scores = jnp.einsum(
        "xrz,frz->rxf", query_head_rows, key_head_rows, preferred_element_type=jnp.float32
    ) * HEAD_DIM ** (-0.5)
    new_max = jnp.maximum(running_max, jnp.max(scores, axis=2))
    exponent = jnp.exp(scores - new_max[:, :, None])
    running_sum = jnp.sum(exponent, axis=2)
    weighted = jnp.einsum(
        "bau,uby->bay",
        exponent.astype(jnp.bfloat16),
        value_head_rows,
        preferred_element_type=jnp.float32,
    )
    return (new_max, running_sum, weighted)


def finish(state_now):
    running_max, running_sum, weighted = state_now
    result = weighted / running_sum[:, :, None]
    head_count, row_count = running_sum.shape
    return result.transpose(1, 0, 2).reshape(row_count, head_count * HEAD_DIM)


def body(
    ray_tokens,
    up_weight,
    down_weight,
    key_weight,
    value_weight,
    video_queries,
    video_keys,
    video_values,
    cross_queries,
):
    row_count = video_queries.shape[0]
    head_count = video_queries.shape[1] // HEAD_DIM
    up_full, down_full, key_full, value_full = (
        lax.all_gather(up_weight, "dp", axis=0, tiled=True),
        lax.all_gather(down_weight, "dp", axis=0, tiled=True),
        lax.all_gather(key_weight, "dp", axis=0, tiled=True),
        lax.all_gather(value_weight, "dp", axis=0, tiled=True),
    )
    normed = rms_normed(ray_tokens).astype(jnp.bfloat16)
    hidden = jax.nn.gelu(jnp.dot(normed, up_full, preferred_element_type=jnp.float32)).astype(
        jnp.bfloat16
    )
    partial_branch = lax.dot_general(
        hidden, down_full, (((1,), (1,)), ((), ())), preferred_element_type=jnp.float32
    )
    branch = lax.psum(partial_branch, "head")
    rays = (ray_tokens.astype(jnp.float32) + branch).astype(jnp.bfloat16)
    cross_heads = cross_queries.reshape(row_count, head_count, HEAD_DIM)
    piece = lax.all_gather(rays, ("view", "dp"), axis=0, tiled=True)
    piece_keys = jnp.dot(piece, key_full, preferred_element_type=jnp.float32).astype(jnp.bfloat16)
    piece_values = jnp.dot(piece, value_full, preferred_element_type=jnp.float32).astype(
        jnp.bfloat16
    )
    cross_state = absorb(empty_state(head_count, row_count), cross_heads, piece_keys, piece_values)
    cross = finish(cross_state)
    local_head_group = video_queries.reshape(row_count, head_count, HEAD_DIM)
    own_state = absorb(
        empty_state(head_count, row_count),
        local_head_group,
        lax.all_gather(video_keys, ("view", "dp"), axis=0, tiled=True),
        lax.all_gather(video_values, ("view", "dp"), axis=0, tiled=True),
    )
    own = finish(own_state)
    return (own + cross).astype(jnp.bfloat16)


MESH = pl.DeviceIdType.MESH
QUERY_BLOCK = 256
FIRST_HEADS = 2
SECOND_HEADS = 1
NOT_DEFERRED = 1
SENT_AHEAD = 2


def softmax_mix(queries, keys, values):
    scores = lax.dot_general(
        queries, keys, (((1,), (1,)), ((), ())), preferred_element_type=jnp.float32
    )
    largest = jnp.max(scores, axis=1, keepdims=True)
    weights = jnp.exp((scores - largest) * HEAD_DIM ** (-0.5))
    row_sums = jnp.sum(weights, axis=1, keepdims=True)
    mixed = jnp.dot(weights.astype(jnp.bfloat16), values, preferred_element_type=jnp.float32)
    return mixed / row_sums


def columns_of(index):
    return pl.ds(pl.multiple_of(index * HEAD_DIM, HEAD_DIM), HEAD_DIM)


def kernel(
    views,
    head_parts,
    ray_ref,
    up_ref,
    down_ref,
    key_ref,
    value_ref,
    query_ref,
    video_key_ref,
    video_value_ref,
    cross_query_ref,
    own_ref,
    cross_out_ref,
    up_full,
    down_full,
    key_full,
    value_full,
    cross_queries,
    ray_tokens,
    hidden_ref,
    partials_out,
    partials_in,
    rays,
    query_heads,
    pair_heads,
    own_heads,
    cross_ref,
    weight_local,
    weight_send,
    weight_recv,
    query_recv,
    pair_recv,
    relay_recv,
    bulk_send,
    relay_send,
    partial_send,
    partial_recv,
    ray_send,
    ray_recv,
    share_send,
    share_recv,
    pair_ray_send,
    pair_ray_recv,
    own_send,
    own_recv,
    own_local,
    cross_sem,
    view_greeted,
    part_greeted,
    core_greeted,
):
    view = lax.axis_index("view")
    part = lax.axis_index("head")
    core = lax.axis_index("dp")
    other = 1 - core
    rows = query_ref.shape[0]
    head_count = query_ref.shape[1] // HEAD_DIM
    per_view = head_count // views
    ray_rows = ray_ref.shape[0]
    half = up_ref.shape[0]
    inner = up_ref.shape[1]
    share = ray_ref.shape[1] // head_parts
    side = views // 2

    peers = [lax.rem(view + step, views) for step in range(1, views)]
    part_peers = [lax.rem(part + step, head_parts) for step in range(1, head_parts)]

    ordered_peers = [jnp.where(step < view, view - 1 - step, step + 1) for step in range(views - 1)]

    barrier = pltpu.get_barrier_semaphore()

    def enter(axis, peer, first):
        @pl.when(first)
        def _():
            pl.semaphore_signal(barrier, inc=1, device_id={axis: peer}, device_id_type=MESH)

    def answer(axis, peer, position, greeted, second):
        @pl.when(second)
        def _():
            pl.semaphore_signal(
                greeted.at[position], inc=1, device_id={axis: peer}, device_id_type=MESH
            )

    for peer in ordered_peers:
        enter("view", peer, view < peer)
    for peer in part_peers:
        enter("head", peer, part < peer)
    enter("dp", other, core == 1)
    earlier = view + part + other

    @pl.when(earlier > 0)
    def _():
        pl.semaphore_wait(barrier, earlier)

    for peer in ordered_peers:
        answer("view", peer, view, view_greeted, view > peer)
    for peer in part_peers:
        answer("head", peer, part, part_greeted, part > peer)
    answer("dp", other, core, core_greeted, core == 0)

    depth = pl.ds(pl.multiple_of(core * half, half), half)
    weight_pairs = (
        (up_ref, up_full.at[core]),
        (down_ref, down_full.at[core]),
        (key_ref, key_full.at[depth]),
        (value_ref, value_full.at[depth]),
    )
    local_copies = [
        pltpu.make_async_copy(source, slot, weight_local.at[index])
        for index, (source, slot) in enumerate(weight_pairs)
    ]
    local_copies.append(
        pltpu.make_async_copy(cross_query_ref, cross_queries, weight_local.at[4])
    )
    remote_copies = [
        pltpu.make_async_remote_copy(
            src_ref=source,
            dst_ref=slot,
            send_sem=weight_send.at[index],
            recv_sem=weight_recv.at[index],
            device_id={"dp": other},
            device_id_type=MESH,
        )
        for index, (source, slot) in enumerate(weight_pairs)
    ]
    local_copies.append(pltpu.make_async_copy(ray_ref, ray_tokens, weight_local.at[5]))
    own_rows = pl.ds(pl.multiple_of(view * rows, rows), rows)

    def keep_heads(index, carry):
        columns = columns_of(view * per_view + index)
        pltpu.make_async_copy(
            query_ref.at[:, columns], query_heads.at[index, own_rows], query_recv.at[index]
        ).start()
        pltpu.make_async_copy(
            video_key_ref.at[:, columns],
            pair_heads.at[index, core, 0, own_rows],
            pair_recv.at[index],
        ).start()
        pltpu.make_async_copy(
            video_value_ref.at[:, columns],
            pair_heads.at[index, core, 1, own_rows],
            pair_recv.at[index],
        ).start()
        return carry


    def send_head(index, peer):
        columns = columns_of(peer * per_view + index)
        for tensor, (source, target, arrived) in enumerate((
            (video_key_ref, pair_heads.at[index, core, 0, own_rows], pair_recv.at[index]),
            (video_value_ref, pair_heads.at[index, core, 1, own_rows], pair_recv.at[index]),
            (query_ref, query_heads.at[index, own_rows], query_recv.at[index]),
        )):
            pltpu.make_async_remote_copy(
                src_ref=source.at[:, columns],
                dst_ref=target,
                send_sem=bulk_send.at[tensor],
                recv_sem=arrived,
                device_id={"view": peer},
                device_id_type=MESH,
            ).start()

    def send_heads(index, carry):
        for peer in peers:
            send_head(index, peer)
        return carry

    first_heads = min(FIRST_HEADS, per_view)
    for step, peer in enumerate(ordered_peers):
        @pl.when(step >= view)
        def _():
            pl.semaphore_wait(view_greeted.at[step + 1], 1)

        def send_first(index, carry):
            send_head(index, peer)
            return carry

        lax.fori_loop(0, first_heads, send_first, 0)

    @pl.when(core == 1)
    def _():
        pl.semaphore_wait(core_greeted.at[0], 1)

    for copy in remote_copies[:2]:
        copy.start()
    for copy in local_copies[::-1]:
        copy.start()
    lax.fori_loop(0, per_view, keep_heads, 0)
    for copy in remote_copies[2:]:
        copy.start()

    local_copies[5].wait()
    tokens = ray_tokens[...]
    normed = rms_normed(tokens).astype(jnp.bfloat16)
    local_copies[0].wait()
    remote_copies[0].wait_recv()
    tile = min(512, inner)

    def up_tile(index, carry):
        columns = pl.ds(pl.multiple_of(index * tile, tile), tile)
        total = jnp.dot(normed[:, :half], up_full[0, :, columns], preferred_element_type=jnp.float32)
        total += jnp.dot(normed[:, half:], up_full[1, :, columns], preferred_element_type=jnp.float32)
        hidden_ref[:, columns] = jax.nn.gelu(total).astype(jnp.bfloat16)
        return carry

    lax.fori_loop(0, inner // tile, up_tile, 0)
    local_copies[1].wait()
    remote_copies[1].wait_recv()
    branch = jnp.concatenate(
        [
            lax.dot_general(
                hidden_ref[...],
                down_full[index],
                (((1,), (1,)), ((), ())),
                preferred_element_type=jnp.float32,
            )
            for index in range(2)
        ],
        axis=1,
    )
    for index in range(head_parts):
        partials_out[index] = branch[:, index * share : (index + 1) * share]
    partial_copies = [
        pltpu.make_async_remote_copy(
            src_ref=partials_out.at[peer],
            dst_ref=partials_in.at[step],
            send_sem=partial_send.at[step],
            recv_sem=partial_recv.at[step],
            device_id={"head": peer},
            device_id_type=MESH,
        )
        for step, peer in enumerate(part_peers)
    ]
    for later in range(1, head_parts):
        @pl.when(part < later)
        def _():
            pl.semaphore_wait(part_greeted.at[later], 1)

    for copy in partial_copies:
        copy.start()
    for copy in partial_copies:
        copy.wait_recv()
    total_share = partials_out[part]
    for index in range(head_parts - 1):
        total_share += partials_in[index]
    share_columns = pl.ds(pl.multiple_of(part * share, share), share)
    rays[core, part, view] = (
        ray_tokens[:, share_columns].astype(jnp.float32) + total_share
    ).astype(jnp.bfloat16)
    side_start = (view // side) * side
    far_start = side - side_start
    gate = jnp.where(side_start == 0, side - 1, side)
    far_gate = 2 * side - 1 - gate
    side_peers = [side_start + lax.rem(view - side_start + step, side) for step in range(1, side)]

    def ray_copy(source, peer, index, arrived):
        return pltpu.make_async_remote_copy(
            src_ref=source,
            dst_ref=source,
            send_sem=ray_send.at[index],
            recv_sem=ray_recv.at[arrived],
            device_id={"view": peer},
            device_id_type=MESH,
        )

    mine = rays.at[core, part, view]
    far_slots = rays.at[core, part, pl.ds(far_start, side)]
    ray_copies = [ray_copy(mine, peer, step, step) for step, peer in enumerate(side_peers)]
    far_copy = ray_copy(mine, far_gate, side - 1, side - 1)
    far_copy.start()
    for copy in ray_copies:
        copy.start()
    second_heads = min(first_heads + SECOND_HEADS, per_view)
    facing_view = jnp.logical_or(view == side - 1, view == side)

    @pl.when(facing_view)
    def _():
        lax.fori_loop(first_heads, second_heads, send_heads, 0)


    def relay(index):
        return pltpu.make_async_remote_copy(
            src_ref=pair_heads.at[index, core],
            dst_ref=pair_heads.at[index, core],
            send_sem=relay_send.at[index],
            recv_sem=relay_recv.at[index],
            device_id={"dp": other},
            device_id_type=MESH,
        )

    def pass_on(index, carry):
        arrived = pair_heads.at[index, core]
        pltpu.make_async_copy(arrived, arrived, pair_recv.at[index]).wait()
        relay(index).start()
        return carry

    last_view = far_start + side - 1

    def own_copy(index, peer):
        return pltpu.make_async_remote_copy(
            src_ref=own_heads.at[index, pl.ds(pl.multiple_of(peer * rows, rows), rows)],
            dst_ref=own_ref.at[:, columns_of(view * per_view + index)],
            send_sem=own_send,
            recv_sem=own_recv,
            device_id={"view": peer},
            device_id_type=MESH,
        )

    def send_last(index, carry):
        own_copy(index, last_view).start()
        return carry

    def attend(index, carry):
        arrived = query_heads.at[index]
        pltpu.make_async_copy(arrived, arrived, query_recv.at[index]).wait()
        relay(index).wait_recv()
        keys = pair_heads[index, :, 0].reshape(2 * views * rows, HEAD_DIM)
        values = pair_heads[index, :, 1].reshape(2 * views * rows, HEAD_DIM)
        block = min(QUERY_BLOCK, views * rows)

        def attend_block(piece, inner_carry):
            span = pl.ds(pl.multiple_of(piece * block, block), block)
            own_heads[index, span] = softmax_mix(query_heads[index, span], keys, values).astype(
                jnp.bfloat16
            )
            return inner_carry

        lax.fori_loop(0, views * rows // block, attend_block, 0)
        columns = columns_of(view * per_view + index)
        pltpu.make_async_copy(
            own_heads.at[index, own_rows], own_ref.at[:, columns], own_local
        ).start()
        for peer in peers:
            @pl.when(jnp.logical_or(index < NOT_DEFERRED, peer != last_view))
            def _():
                own_copy(index, peer).start()

        return carry

    lax.fori_loop(0, 1, pass_on, 0)

    @pl.when(jnp.logical_not(facing_view))
    def _():
        lax.fori_loop(first_heads, second_heads, send_heads, 0)

    lax.fori_loop(1, first_heads, pass_on, 0)
    pltpu.make_async_copy(far_slots, far_slots, ray_recv.at[side - 1]).wait()
    gate_copies = [
        ray_copy(far_slots, peer, side + step, side - 1) for step, peer in enumerate(side_peers)
    ]

    @pl.when(view == gate)
    def _():
        for copy in gate_copies:
            copy.start()

    lax.fori_loop(second_heads, per_view, send_heads, 0)
    for copy in ray_copies:
        copy.wait_recv()
    share_copies = [
        pltpu.make_async_remote_copy(
            src_ref=rays.at[core, part],
            dst_ref=rays.at[core, part],
            send_sem=share_send.at[step],
            recv_sem=share_recv.at[step],
            device_id={"head": peer},
            device_id_type=MESH,
        )
        for step, peer in enumerate(part_peers)
    ]
    for copy in share_copies:
        copy.start()
    lax.fori_loop(0, first_heads, attend, 0)
    lax.fori_loop(first_heads, second_heads, pass_on, 0)
    for copy in share_copies:
        copy.wait_recv()
    ray_relay = pltpu.make_async_remote_copy(
        src_ref=rays.at[core],
        dst_ref=rays.at[core],
        send_sem=pair_ray_send,
        recv_sem=pair_ray_recv,
        device_id={"dp": other},
        device_id_type=MESH,
    )
    ray_relay.start()
    lax.fori_loop(first_heads, second_heads, attend, 0)

    ray_relay.wait_recv()
    for index in (2, 3):
        local_copies[index].wait()
        remote_copies[index].wait_recv()
    local_copies[4].wait()
    ray_shares = [
        rays[:, index].reshape(2 * views * ray_rows, share) for index in range(head_parts)
    ]
    group = 2 if head_count % 2 == 0 else 1
    width = group * HEAD_DIM

    def cross_group(index, carry):
        columns = pl.ds(pl.multiple_of(index * width, width), width)

        def project(full):
            total = 0.0
            for index, ray_share in enumerate(ray_shares):
                total += jnp.dot(
                    ray_share,
                    full[index * share : (index + 1) * share, columns],
                    preferred_element_type=jnp.float32,
                )
            return total.astype(jnp.bfloat16)

        keys, values = project(key_full), project(value_full)
        queries = cross_queries[:, columns]
        results = []
        for lane in range(group):
            span = slice(lane * HEAD_DIM, (lane + 1) * HEAD_DIM)
            results.append(softmax_mix(queries[:, span], keys[:, span], values[:, span]))
        cross_ref[:, columns] = jnp.concatenate(results, axis=1)
        return carry

    lax.fori_loop(0, head_count // group, cross_group, 0)
    cross_copy = pltpu.make_async_copy(cross_ref, cross_out_ref, cross_sem)
    cross_copy.start()

    lax.fori_loop(second_heads, per_view, pass_on, 0)
    last_head = max(second_heads, per_view - 1)
    middle = min(SENT_AHEAD, per_view)
    lax.fori_loop(second_heads, last_head, attend, 0)
    lax.fori_loop(NOT_DEFERRED, middle, send_last, 0)
    lax.fori_loop(last_head, per_view, attend, 0)
    lax.fori_loop(middle, per_view, send_last, 0)

    sent_copies = remote_copies + partial_copies + ray_copies + share_copies
    for copy in sent_copies + [far_copy, ray_relay]:
        copy.wait_send()

    @pl.when(view == gate)
    def _():
        for copy in gate_copies:
            copy.wait_send()

    def relay_sent(index, carry):
        relay(index).wait_send()
        return carry

    lax.fori_loop(0, per_view, relay_sent, 0)
    for tensor in range(3):
        sent = query_heads.at[:, pl.ds(0, (views - 1) * rows)]
        pltpu.make_async_copy(sent, sent, bulk_send.at[tensor]).wait()
    cross_copy.wait()
    kept = own_heads.at[:, pl.ds(0, rows)]
    pltpu.make_async_copy(kept, kept, own_local).wait()
    returned = own_heads.at[:, pl.ds(0, (views - 1) * rows)]
    pltpu.make_async_copy(returned, returned, own_send).wait()
    pltpu.make_async_copy(returned, returned, own_recv).wait()


def fused_body(views, head_parts, *args):
    ray_tokens, up_weight, down_weight, key_weight, value_weight, video_queries = args[:6]
    rows, columns = video_queries.shape
    per_view = columns // HEAD_DIM // views
    ray_rows, ray_width = ray_tokens.shape
    half, inner = up_weight.shape
    share = ray_width // head_parts
    bf16, f32 = jnp.bfloat16, jnp.float32
    dma = pltpu.SemaphoreType.DMA
    anywhere = pl.BlockSpec(memory_space=pl.ANY)
    args = [pltpu.with_memory_space_constraint(arg, pltpu.HBM) for arg in args]
    own, cross = pl.pallas_call(
        functools.partial(kernel, views, head_parts),
        out_shape=(pltpu.VMEM((rows, columns), bf16), pltpu.VMEM((rows, columns), f32)),
        in_specs=[anywhere] * 9,
        out_specs=(anywhere, anywhere),
        scratch_shapes=[
            pltpu.VMEM((2,) + up_weight.shape, bf16),
            pltpu.VMEM((2,) + down_weight.shape, bf16),
            pltpu.VMEM((2 * half, columns), bf16),
            pltpu.VMEM((2 * half, columns), bf16),
            pltpu.VMEM((rows, columns), bf16),
            pltpu.VMEM((ray_rows, ray_width), bf16),
            pltpu.VMEM((ray_rows, inner), bf16),
            pltpu.VMEM((head_parts, ray_rows, share), f32),
            pltpu.VMEM((head_parts, ray_rows, share), f32),
            pltpu.VMEM((2, head_parts, views, ray_rows, share), bf16),
            pltpu.VMEM((per_view, views * rows, HEAD_DIM), bf16),
            pltpu.VMEM((per_view, 2, 2, views * rows, HEAD_DIM), bf16),
            pltpu.VMEM((per_view, views * rows, HEAD_DIM), bf16),
            pltpu.VMEM((rows, columns), f32),
            dma((6,)),
            dma((4,)),
            dma((4,)),
            dma((per_view,)),
            dma((per_view,)),
            dma((per_view,)),
            dma((3,)),
            dma((per_view,)),
            dma((max(head_parts - 1, 1),)),
            dma((max(head_parts - 1, 1),)),
            dma((views,)),
            dma((views,)),
            dma((max(head_parts - 1, 1),)),
            dma((max(head_parts - 1, 1),)),
            dma,
            dma,
            dma,
            dma,
            dma,
            dma,
            pltpu.SemaphoreType.REGULAR((views,)),
            pltpu.SemaphoreType.REGULAR((head_parts,)),
            pltpu.SemaphoreType.REGULAR((2,)),
        ],
        compiler_params=pltpu.CompilerParams(
            collective_id=0, has_side_effects=True, vmem_limit_bytes=48 * 2**20
        ),
    )(*args)
    return (cross + own.astype(f32)).astype(bf16)


def solution(mesh):
    views, head_parts = mesh.shape["view"], mesh.shape["head"]

    def routed(*args):
        head_count = args[5].shape[1] // HEAD_DIM
        if (
            mesh.shape["dp"] == 2
            and views % 2 == 0
            and head_count % views == 0
            and args[0].shape[1] % (head_parts * HEAD_DIM) == 0
        ):
            return fused_body(views, head_parts, *args)
        return body(*args)

    in_specs = (
        P(("groups", "view", "dp"), None),
        P("dp", "head"),
        P("dp", "head"),
        P("dp", "head"),
        P("dp", "head"),
        P(("groups", "view", "dp"), "head"),
        P(("groups", "view", "dp"), "head"),
        P(("groups", "view", "dp"), "head"),
        P(("groups", "view", "dp"), "head"),
    )
    out_specs = P(("groups", "view", "dp"), "head")
    return jax.shard_map(routed, mesh=mesh, in_specs=in_specs, out_specs=out_specs, check_vma=False)
```

```python
import functools

import jax
import jax.numpy as jnp
from jax import lax
from jax.experimental import pallas as pl
from jax.experimental.pallas import tpu as pltpu
from jax.sharding import PartitionSpec as P

HEAD_DIM = 128


epsilon = 1e-06


def rms_normed(values_in):
    widened = values_in.astype(jnp.float32)
    mean_square = jnp.mean(widened * widened, axis=1, keepdims=True)
    return widened * lax.rsqrt(mean_square + epsilon)


def empty_state(head_count, row_count):
    running_max = jnp.full((head_count, row_count), -1e30, jnp.float32)
    running_sum = jnp.zeros((head_count, row_count), jnp.float32)
    weighted = jnp.zeros((head_count, row_count, HEAD_DIM), jnp.float32)
    return (running_max, running_sum, weighted)


def absorb(state_now, query_head_rows, key_piece, value_piece):
    running_max, running_sum, weighted = state_now
    head_count = query_head_rows.shape[1]
    key_head_rows = key_piece.reshape(key_piece.shape[0], head_count, HEAD_DIM)
    value_head_rows = value_piece.reshape(value_piece.shape[0], head_count, HEAD_DIM)
    scores = jnp.einsum(
        "xrz,frz->rxf", query_head_rows, key_head_rows, preferred_element_type=jnp.float32
    ) * HEAD_DIM ** (-0.5)
    new_max = jnp.maximum(running_max, jnp.max(scores, axis=2))
    exponent = jnp.exp(scores - new_max[:, :, None])
    running_sum = jnp.sum(exponent, axis=2)
    weighted = jnp.einsum(
        "bau,uby->bay",
        exponent.astype(jnp.bfloat16),
        value_head_rows,
        preferred_element_type=jnp.float32,
    )
    return (new_max, running_sum, weighted)


def finish(state_now):
    running_max, running_sum, weighted = state_now
    result = weighted / running_sum[:, :, None]
    head_count, row_count = running_sum.shape
    return result.transpose(1, 0, 2).reshape(row_count, head_count * HEAD_DIM)


def body(
    ray_tokens,
    up_weight,
    down_weight,
    key_weight,
    value_weight,
    video_queries,
    video_keys,
    video_values,
    cross_queries,
):
    row_count = video_queries.shape[0]
    head_count = video_queries.shape[1] // HEAD_DIM
    up_full, down_full, key_full, value_full = (
        lax.all_gather(up_weight, "dp", axis=0, tiled=True),
        lax.all_gather(down_weight, "dp", axis=0, tiled=True),
        lax.all_gather(key_weight, "dp", axis=0, tiled=True),
        lax.all_gather(value_weight, "dp", axis=0, tiled=True),
    )
    normed = rms_normed(ray_tokens).astype(jnp.bfloat16)
    hidden = jax.nn.gelu(jnp.dot(normed, up_full, preferred_element_type=jnp.float32)).astype(
        jnp.bfloat16
    )
    partial_branch = lax.dot_general(
        hidden, down_full, (((1,), (1,)), ((), ())), preferred_element_type=jnp.float32
    )
    branch = lax.psum(partial_branch, "head")
    rays = (ray_tokens.astype(jnp.float32) + branch).astype(jnp.bfloat16)
    cross_heads = cross_queries.reshape(row_count, head_count, HEAD_DIM)
    piece = lax.all_gather(rays, ("view", "dp"), axis=0, tiled=True)
    piece_keys = jnp.dot(piece, key_full, preferred_element_type=jnp.float32).astype(jnp.bfloat16)
    piece_values = jnp.dot(piece, value_full, preferred_element_type=jnp.float32).astype(
        jnp.bfloat16
    )
    cross_state = absorb(empty_state(head_count, row_count), cross_heads, piece_keys, piece_values)
    cross = finish(cross_state)
    local_head_group = video_queries.reshape(row_count, head_count, HEAD_DIM)
    own_state = absorb(
        empty_state(head_count, row_count),
        local_head_group,
        lax.all_gather(video_keys, ("view", "dp"), axis=0, tiled=True),
        lax.all_gather(video_values, ("view", "dp"), axis=0, tiled=True),
    )
    own = finish(own_state)
    return (own + cross).astype(jnp.bfloat16)


MESH = pl.DeviceIdType.MESH
QUERY_BLOCK = 256
FIRST_HEADS = 2
SECOND_HEADS = 1
NOT_DEFERRED = 1
SENT_AHEAD = 2


def softmax_mix(queries, keys, values):
    scores = lax.dot_general(
        queries, keys, (((1,), (1,)), ((), ())), preferred_element_type=jnp.float32
    )
    largest = jnp.max(scores, axis=1, keepdims=True)
    weights = jnp.exp((scores - largest) * HEAD_DIM ** (-0.5))
    row_sums = jnp.sum(weights, axis=1, keepdims=True)
    mixed = jnp.dot(weights.astype(jnp.bfloat16), values, preferred_element_type=jnp.float32)
    return mixed / row_sums


def columns_of(index):
    return pl.ds(pl.multiple_of(index * HEAD_DIM, HEAD_DIM), HEAD_DIM)


def kernel(
    views,
    head_parts,
    ray_ref,
    up_ref,
    down_ref,
    key_ref,
    value_ref,
    query_ref,
    video_key_ref,
    video_value_ref,
    cross_query_ref,
    own_ref,
    cross_out_ref,
    up_full,
    down_full,
    key_full,
    value_full,
    cross_queries,
    ray_tokens,
    hidden_ref,
    partials_out,
    partials_in,
    rays,
    query_heads,
    pair_heads,
    own_heads,
    cross_ref,
    weight_local,
    weight_send,
    weight_recv,
    query_recv,
    pair_recv,
    relay_recv,
    bulk_send,
    relay_send,
    partial_send,
    partial_recv,
    ray_send,
    ray_recv,
    share_send,
    share_recv,
    pair_ray_send,
    pair_ray_recv,
    own_send,
    own_recv,
    own_local,
    cross_sem,
    view_greeted,
    part_greeted,
    core_greeted,
):
    view = lax.axis_index("view")
    part = lax.axis_index("head")
    core = lax.axis_index("dp")
    other = 1 - core
    rows = query_ref.shape[0]
    head_count = query_ref.shape[1] // HEAD_DIM
    per_view = head_count // views
    ray_rows = ray_ref.shape[0]
    half = up_ref.shape[0]
    inner = up_ref.shape[1]
    share = ray_ref.shape[1] // head_parts
    side = views // 2

    peers = [lax.rem(view + step, views) for step in range(1, views)]
    part_peers = [lax.rem(part + step, head_parts) for step in range(1, head_parts)]

    ordered_peers = [jnp.where(step < view, view - 1 - step, step + 1) for step in range(views - 1)]

    barrier = pltpu.get_barrier_semaphore()

    def enter(axis, peer, first):
        @pl.when(first)
        def _():
            pl.semaphore_signal(barrier, inc=1, device_id={axis: peer}, device_id_type=MESH)

    def answer(axis, peer, position, greeted, second):
        @pl.when(second)
        def _():
            pl.semaphore_signal(
                greeted.at[position], inc=1, device_id={axis: peer}, device_id_type=MESH
            )

    for peer in part_peers:
        enter("head", peer, part < peer)
    enter("dp", other, core == 1)
    for peer in ordered_peers:
        enter("view", peer, view < peer)
    earlier = view + part + other

    @pl.when(earlier > 0)
    def _():
        pl.semaphore_wait(barrier, earlier)

    for peer in ordered_peers:
        answer("view", peer, view, view_greeted, view > peer)
    for peer in part_peers:
        answer("head", peer, part, part_greeted, part > peer)
    answer("dp", other, core, core_greeted, core == 0)

    depth = pl.ds(pl.multiple_of(core * half, half), half)
    weight_pairs = (
        (up_ref, up_full.at[core]),
        (down_ref, down_full.at[core]),
        (key_ref, key_full.at[depth]),
        (value_ref, value_full.at[depth]),
    )
    local_copies = [
        pltpu.make_async_copy(source, slot, weight_local.at[index])
        for index, (source, slot) in enumerate(weight_pairs)
    ]
    local_copies.append(
        pltpu.make_async_copy(cross_query_ref, cross_queries, weight_local.at[4])
    )
    remote_copies = [
        pltpu.make_async_remote_copy(
            src_ref=source,
            dst_ref=slot,
            send_sem=weight_send.at[index],
            recv_sem=weight_recv.at[index],
            device_id={"dp": other},
            device_id_type=MESH,
        )
        for index, (source, slot) in enumerate(weight_pairs)
    ]
    local_copies.append(pltpu.make_async_copy(ray_ref, ray_tokens, weight_local.at[5]))
    own_rows = pl.ds(pl.multiple_of(view * rows, rows), rows)

    def keep_heads(index, carry):
        columns = columns_of(view * per_view + index)
        pltpu.make_async_copy(
            query_ref.at[:, columns], query_heads.at[index, own_rows], query_recv.at[index]
        ).start()
        pltpu.make_async_copy(
            video_key_ref.at[:, columns],
            pair_heads.at[index, core, 0, own_rows],
            pair_recv.at[index],
        ).start()
        pltpu.make_async_copy(
            video_value_ref.at[:, columns],
            pair_heads.at[index, core, 1, own_rows],
            pair_recv.at[index],
        ).start()
        return carry


    def send_head(index, peer):
        columns = columns_of(peer * per_view + index)
        for tensor, (source, target, arrived) in enumerate((
            (video_key_ref, pair_heads.at[index, core, 0, own_rows], pair_recv.at[index]),
            (video_value_ref, pair_heads.at[index, core, 1, own_rows], pair_recv.at[index]),
            (query_ref, query_heads.at[index, own_rows], query_recv.at[index]),
        )):
            pltpu.make_async_remote_copy(
                src_ref=source.at[:, columns],
                dst_ref=target,
                send_sem=bulk_send.at[tensor],
                recv_sem=arrived,
                device_id={"view": peer},
                device_id_type=MESH,
            ).start()

    def send_heads(index, carry):
        for peer in peers:
            send_head(index, peer)
        return carry

    first_heads = min(FIRST_HEADS, per_view)
    for step, peer in enumerate(ordered_peers):
        @pl.when(step >= view)
        def _():
            pl.semaphore_wait(view_greeted.at[step + 1], 1)

        def send_first(index, carry):
            send_head(index, peer)
            return carry

        lax.fori_loop(0, first_heads, send_first, 0)

    @pl.when(core == 1)
    def _():
        pl.semaphore_wait(core_greeted.at[0], 1)

    for copy in remote_copies[:2]:
        copy.start()
    for copy in local_copies[::-1]:
        copy.start()
    lax.fori_loop(0, per_view, keep_heads, 0)
    for copy in remote_copies[2:]:
        copy.start()

    local_copies[5].wait()
    tokens = ray_tokens[...]
    normed = rms_normed(tokens).astype(jnp.bfloat16)
    local_copies[0].wait()
    remote_copies[0].wait_recv()
    tile = min(512, inner)

    def up_tile(index, carry):
        columns = pl.ds(pl.multiple_of(index * tile, tile), tile)
        total = jnp.dot(normed[:, :half], up_full[0, :, columns], preferred_element_type=jnp.float32)
        total += jnp.dot(normed[:, half:], up_full[1, :, columns], preferred_element_type=jnp.float32)
        hidden_ref[:, columns] = jax.nn.gelu(total).astype(jnp.bfloat16)
        return carry

    lax.fori_loop(0, inner // tile, up_tile, 0)
    local_copies[1].wait()
    remote_copies[1].wait_recv()
    branch = jnp.concatenate(
        [
            lax.dot_general(
                hidden_ref[...],
                down_full[index],
                (((1,), (1,)), ((), ())),
                preferred_element_type=jnp.float32,
            )
            for index in range(2)
        ],
        axis=1,
    )
    for index in range(head_parts):
        partials_out[index] = branch[:, index * share : (index + 1) * share]
    partial_copies = [
        pltpu.make_async_remote_copy(
            src_ref=partials_out.at[peer],
            dst_ref=partials_in.at[step],
            send_sem=partial_send.at[step],
            recv_sem=partial_recv.at[step],
            device_id={"head": peer},
            device_id_type=MESH,
        )
        for step, peer in enumerate(part_peers)
    ]
    for later in range(1, head_parts):
        @pl.when(part < later)
        def _():
            pl.semaphore_wait(part_greeted.at[later], 1)

    for copy in partial_copies:
        copy.start()
    for copy in partial_copies:
        copy.wait_recv()
    total_share = partials_out[part]
    for index in range(head_parts - 1):
        total_share += partials_in[index]
    share_columns = pl.ds(pl.multiple_of(part * share, share), share)
    rays[core, part, view] = (
        ray_tokens[:, share_columns].astype(jnp.float32) + total_share
    ).astype(jnp.bfloat16)
    side_start = (view // side) * side
    far_start = side - side_start
    gate = jnp.where(side_start == 0, side - 1, side)
    far_gate = 2 * side - 1 - gate
    side_peers = [side_start + lax.rem(view - side_start + step, side) for step in range(1, side)]

    def ray_copy(source, peer, index, arrived):
        return pltpu.make_async_remote_copy(
            src_ref=source,
            dst_ref=source,
            send_sem=ray_send.at[index],
            recv_sem=ray_recv.at[arrived],
            device_id={"view": peer},
            device_id_type=MESH,
        )

    mine = rays.at[core, part, view]
    far_slots = rays.at[core, part, pl.ds(far_start, side)]
    ray_copies = [ray_copy(mine, peer, step, step) for step, peer in enumerate(side_peers)]
    far_copy = ray_copy(mine, far_gate, side - 1, side - 1)
    far_copy.start()
    for copy in ray_copies:
        copy.start()
    second_heads = min(first_heads + SECOND_HEADS, per_view)
    facing_view = jnp.logical_or(view == side - 1, view == side)

    @pl.when(facing_view)
    def _():
        lax.fori_loop(first_heads, second_heads, send_heads, 0)


    def relay(index):
        return pltpu.make_async_remote_copy(
            src_ref=pair_heads.at[index, core],
            dst_ref=pair_heads.at[index, core],
            send_sem=relay_send.at[index],
            recv_sem=relay_recv.at[index],
            device_id={"dp": other},
            device_id_type=MESH,
        )

    def pass_on(index, carry):
        arrived = pair_heads.at[index, core]
        pltpu.make_async_copy(arrived, arrived, pair_recv.at[index]).wait()
        relay(index).start()
        return carry

    last_view = far_start + side - 1

    def own_copy(index, peer):
        return pltpu.make_async_remote_copy(
            src_ref=own_heads.at[index, pl.ds(pl.multiple_of(peer * rows, rows), rows)],
            dst_ref=own_ref.at[:, columns_of(view * per_view + index)],
            send_sem=own_send,
            recv_sem=own_recv,
            device_id={"view": peer},
            device_id_type=MESH,
        )

    def send_last(index, carry):
        own_copy(index, last_view).start()
        return carry

    holds = jnp.logical_not(facing_view)

    def not_last(index, peer):
        return jnp.logical_or(index < NOT_DEFERRED, peer != last_view)

    def attend(index, carry):
        arrived = query_heads.at[index]
        pltpu.make_async_copy(arrived, arrived, query_recv.at[index]).wait()
        relay(index).wait_recv()
        keys = pair_heads[index, :, 0].reshape(2 * views * rows, HEAD_DIM)
        values = pair_heads[index, :, 1].reshape(2 * views * rows, HEAD_DIM)
        block = min(QUERY_BLOCK, views * rows)

        def attend_block(piece, inner_carry):
            span = pl.ds(pl.multiple_of(piece * block, block), block)
            own_heads[index, span] = softmax_mix(query_heads[index, span], keys, values).astype(
                jnp.bfloat16
            )
            return inner_carry

        lax.fori_loop(0, views * rows // block, attend_block, 0)
        columns = columns_of(view * per_view + index)
        pltpu.make_async_copy(
            own_heads.at[index, own_rows], own_ref.at[:, columns], own_local
        ).start()
        for peer in peers:
            held = jnp.logical_and(
                jnp.logical_and(holds, index < second_heads), peer // side != view // side
            )

            @pl.when(jnp.logical_and(not_last(index, peer), jnp.logical_not(held)))
            def _():
                own_copy(index, peer).start()

        return carry

    def send_held(index, carry):
        for peer in peers:
            far = peer // side != view // side

            @pl.when(jnp.logical_and(not_last(index, peer), far))
            def _():
                own_copy(index, peer).start()

        return carry

    lax.fori_loop(0, 1, pass_on, 0)

    @pl.when(jnp.logical_not(facing_view))
    def _():
        lax.fori_loop(first_heads, second_heads, send_heads, 0)

    lax.fori_loop(1, first_heads, pass_on, 0)
    pltpu.make_async_copy(far_slots, far_slots, ray_recv.at[side - 1]).wait()
    gate_copies = [
        ray_copy(far_slots, peer, side + step, side - 1) for step, peer in enumerate(side_peers)
    ]

    @pl.when(view == gate)
    def _():
        for copy in gate_copies:
            copy.start()

    lax.fori_loop(second_heads, per_view, send_heads, 0)
    for copy in ray_copies:
        copy.wait_recv()
    share_copies = [
        pltpu.make_async_remote_copy(
            src_ref=rays.at[core, part],
            dst_ref=rays.at[core, part],
            send_sem=share_send.at[step],
            recv_sem=share_recv.at[step],
            device_id={"head": peer},
            device_id_type=MESH,
        )
        for step, peer in enumerate(part_peers)
    ]
    for copy in share_copies:
        copy.start()
    lax.fori_loop(0, first_heads, attend, 0)
    lax.fori_loop(first_heads, second_heads, pass_on, 0)
    for copy in share_copies:
        copy.wait_recv()
    ray_relay = pltpu.make_async_remote_copy(
        src_ref=rays.at[core],
        dst_ref=rays.at[core],
        send_sem=pair_ray_send,
        recv_sem=pair_ray_recv,
        device_id={"dp": other},
        device_id_type=MESH,
    )
    ray_relay.start()
    lax.fori_loop(first_heads, second_heads, attend, 0)

    ray_relay.wait_recv()
    for index in (2, 3):
        local_copies[index].wait()
        remote_copies[index].wait_recv()
    local_copies[4].wait()
    ray_shares = [
        rays[:, index].reshape(2 * views * ray_rows, share) for index in range(head_parts)
    ]
    group = 2 if head_count % 2 == 0 else 1
    width = group * HEAD_DIM

    def cross_group(index, carry):
        columns = pl.ds(pl.multiple_of(index * width, width), width)

        def project(full):
            total = 0.0
            for index, ray_share in enumerate(ray_shares):
                total += jnp.dot(
                    ray_share,
                    full[index * share : (index + 1) * share, columns],
                    preferred_element_type=jnp.float32,
                )
            return total.astype(jnp.bfloat16)

        keys, values = project(key_full), project(value_full)
        queries = cross_queries[:, columns]
        results = []
        for lane in range(group):
            span = slice(lane * HEAD_DIM, (lane + 1) * HEAD_DIM)
            results.append(softmax_mix(queries[:, span], keys[:, span], values[:, span]))
        cross_ref[:, columns] = jnp.concatenate(results, axis=1)
        return carry

    lax.fori_loop(0, head_count // group, cross_group, 0)
    cross_copy = pltpu.make_async_copy(cross_ref, cross_out_ref, cross_sem)
    cross_copy.start()

    lax.fori_loop(second_heads, per_view, pass_on, 0)

    @pl.when(holds)
    def _():
        lax.fori_loop(0, second_heads, send_held, 0)

    last_head = max(second_heads, per_view - 1)
    sent_ahead = jnp.logical_and(holds, view >= side)
    middle = jnp.where(sent_ahead, min(SENT_AHEAD, per_view), NOT_DEFERRED)
    lax.fori_loop(second_heads, last_head, attend, 0)
    lax.fori_loop(NOT_DEFERRED, middle, send_last, 0)
    lax.fori_loop(last_head, per_view, attend, 0)
    lax.fori_loop(middle, per_view, send_last, 0)

    sent_copies = remote_copies + partial_copies + ray_copies + share_copies
    for copy in sent_copies + [far_copy, ray_relay]:
        copy.wait_send()

    @pl.when(view == gate)
    def _():
        for copy in gate_copies:
            copy.wait_send()

    def relay_sent(index, carry):
        relay(index).wait_send()
        return carry

    lax.fori_loop(0, per_view, relay_sent, 0)
    for tensor in range(3):
        sent = query_heads.at[:, pl.ds(0, (views - 1) * rows)]
        pltpu.make_async_copy(sent, sent, bulk_send.at[tensor]).wait()
    cross_copy.wait()
    kept = own_heads.at[:, pl.ds(0, rows)]
    pltpu.make_async_copy(kept, kept, own_local).wait()
    returned = own_heads.at[:, pl.ds(0, (views - 1) * rows)]
    pltpu.make_async_copy(returned, returned, own_send).wait()
    pltpu.make_async_copy(returned, returned, own_recv).wait()


def fused_body(views, head_parts, *args):
    ray_tokens, up_weight, down_weight, key_weight, value_weight, video_queries = args[:6]
    rows, columns = video_queries.shape
    per_view = columns // HEAD_DIM // views
    ray_rows, ray_width = ray_tokens.shape
    half, inner = up_weight.shape
    share = ray_width // head_parts
    bf16, f32 = jnp.bfloat16, jnp.float32
    dma = pltpu.SemaphoreType.DMA
    anywhere = pl.BlockSpec(memory_space=pl.ANY)
    args = [pltpu.with_memory_space_constraint(arg, pltpu.HBM) for arg in args]
    own, cross = pl.pallas_call(
        functools.partial(kernel, views, head_parts),
        out_shape=(pltpu.VMEM((rows, columns), bf16), pltpu.VMEM((rows, columns), f32)),
        in_specs=[anywhere] * 9,
        out_specs=(anywhere, anywhere),
        scratch_shapes=[
            pltpu.VMEM((2,) + up_weight.shape, bf16),
            pltpu.VMEM((2,) + down_weight.shape, bf16),
            pltpu.VMEM((2 * half, columns), bf16),
            pltpu.VMEM((2 * half, columns), bf16),
            pltpu.VMEM((rows, columns), bf16),
            pltpu.VMEM((ray_rows, ray_width), bf16),
            pltpu.VMEM((ray_rows, inner), bf16),
            pltpu.VMEM((head_parts, ray_rows, share), f32),
            pltpu.VMEM((head_parts, ray_rows, share), f32),
            pltpu.VMEM((2, head_parts, views, ray_rows, share), bf16),
            pltpu.VMEM((per_view, views * rows, HEAD_DIM), bf16),
            pltpu.VMEM((per_view, 2, 2, views * rows, HEAD_DIM), bf16),
            pltpu.VMEM((per_view, views * rows, HEAD_DIM), bf16),
            pltpu.VMEM((rows, columns), f32),
            dma((6,)),
            dma((4,)),
            dma((4,)),
            dma((per_view,)),
            dma((per_view,)),
            dma((per_view,)),
            dma((3,)),
            dma((per_view,)),
            dma((max(head_parts - 1, 1),)),
            dma((max(head_parts - 1, 1),)),
            dma((views,)),
            dma((views,)),
            dma((max(head_parts - 1, 1),)),
            dma((max(head_parts - 1, 1),)),
            dma,
            dma,
            dma,
            dma,
            dma,
            dma,
            pltpu.SemaphoreType.REGULAR((views,)),
            pltpu.SemaphoreType.REGULAR((head_parts,)),
            pltpu.SemaphoreType.REGULAR((2,)),
        ],
        compiler_params=pltpu.CompilerParams(
            collective_id=0, has_side_effects=True, vmem_limit_bytes=48 * 2**20
        ),
    )(*args)
    return (cross + own.astype(f32)).astype(bf16)


def solution(mesh):
    views, head_parts = mesh.shape["view"], mesh.shape["head"]

    def routed(*args):
        head_count = args[5].shape[1] // HEAD_DIM
        if (
            mesh.shape["dp"] == 2
            and views % 2 == 0
            and head_count % views == 0
            and args[0].shape[1] % (head_parts * HEAD_DIM) == 0
        ):
            return fused_body(views, head_parts, *args)
        return body(*args)

    in_specs = (
        P(("groups", "view", "dp"), None),
        P("dp", "head"),
        P("dp", "head"),
        P("dp", "head"),
        P("dp", "head"),
        P(("groups", "view", "dp"), "head"),
        P(("groups", "view", "dp"), "head"),
        P(("groups", "view", "dp"), "head"),
        P(("groups", "view", "dp"), "head"),
    )
    out_specs = P(("groups", "view", "dp"), "head")
    return jax.shard_map(routed, mesh=mesh, in_specs=in_specs, out_specs=out_specs, check_vma=False)
```

```python
import functools

import jax
import jax.numpy as jnp
from jax import lax
from jax.experimental import pallas as pl
from jax.experimental.pallas import tpu as pltpu
from jax.sharding import PartitionSpec as P

HEAD_DIM = 128


epsilon = 1e-06


def rms_normed(values_in):
    widened = values_in.astype(jnp.float32)
    mean_square = jnp.mean(widened * widened, axis=1, keepdims=True)
    return widened * lax.rsqrt(mean_square + epsilon)


def empty_state(head_count, row_count):
    running_max = jnp.full((head_count, row_count), -1e30, jnp.float32)
    running_sum = jnp.zeros((head_count, row_count), jnp.float32)
    weighted = jnp.zeros((head_count, row_count, HEAD_DIM), jnp.float32)
    return (running_max, running_sum, weighted)


def absorb(state_now, query_head_rows, key_piece, value_piece):
    running_max, running_sum, weighted = state_now
    head_count = query_head_rows.shape[1]
    key_head_rows = key_piece.reshape(key_piece.shape[0], head_count, HEAD_DIM)
    value_head_rows = value_piece.reshape(value_piece.shape[0], head_count, HEAD_DIM)
    scores = jnp.einsum(
        "xrz,frz->rxf", query_head_rows, key_head_rows, preferred_element_type=jnp.float32
    ) * HEAD_DIM ** (-0.5)
    new_max = jnp.maximum(running_max, jnp.max(scores, axis=2))
    exponent = jnp.exp(scores - new_max[:, :, None])
    running_sum = jnp.sum(exponent, axis=2)
    weighted = jnp.einsum(
        "bau,uby->bay",
        exponent.astype(jnp.bfloat16),
        value_head_rows,
        preferred_element_type=jnp.float32,
    )
    return (new_max, running_sum, weighted)


def finish(state_now):
    running_max, running_sum, weighted = state_now
    result = weighted / running_sum[:, :, None]
    head_count, row_count = running_sum.shape
    return result.transpose(1, 0, 2).reshape(row_count, head_count * HEAD_DIM)


def body(
    ray_tokens,
    up_weight,
    down_weight,
    key_weight,
    value_weight,
    video_queries,
    video_keys,
    video_values,
    cross_queries,
):
    row_count = video_queries.shape[0]
    head_count = video_queries.shape[1] // HEAD_DIM
    up_full, down_full, key_full, value_full = (
        lax.all_gather(up_weight, "dp", axis=0, tiled=True),
        lax.all_gather(down_weight, "dp", axis=0, tiled=True),
        lax.all_gather(key_weight, "dp", axis=0, tiled=True),
        lax.all_gather(value_weight, "dp", axis=0, tiled=True),
    )
    normed = rms_normed(ray_tokens).astype(jnp.bfloat16)
    hidden = jax.nn.gelu(jnp.dot(normed, up_full, preferred_element_type=jnp.float32)).astype(
        jnp.bfloat16
    )
    partial_branch = lax.dot_general(
        hidden, down_full, (((1,), (1,)), ((), ())), preferred_element_type=jnp.float32
    )
    branch = lax.psum(partial_branch, "head")
    rays = (ray_tokens.astype(jnp.float32) + branch).astype(jnp.bfloat16)
    cross_heads = cross_queries.reshape(row_count, head_count, HEAD_DIM)
    piece = lax.all_gather(rays, ("view", "dp"), axis=0, tiled=True)
    piece_keys = jnp.dot(piece, key_full, preferred_element_type=jnp.float32).astype(jnp.bfloat16)
    piece_values = jnp.dot(piece, value_full, preferred_element_type=jnp.float32).astype(
        jnp.bfloat16
    )
    cross_state = absorb(empty_state(head_count, row_count), cross_heads, piece_keys, piece_values)
    cross = finish(cross_state)
    local_head_group = video_queries.reshape(row_count, head_count, HEAD_DIM)
    own_state = absorb(
        empty_state(head_count, row_count),
        local_head_group,
        lax.all_gather(video_keys, ("view", "dp"), axis=0, tiled=True),
        lax.all_gather(video_values, ("view", "dp"), axis=0, tiled=True),
    )
    own = finish(own_state)
    return (own + cross).astype(jnp.bfloat16)


MESH = pl.DeviceIdType.MESH
QUERY_BLOCK = 256
FIRST_HEADS = 2
SECOND_HEADS = 1
NOT_DEFERRED = 1
SENT_AHEAD = 2
ADD_BLOCKS = 8


def softmax_mix(queries, keys, values):
    scores = lax.dot_general(
        queries, keys, (((1,), (1,)), ((), ())), preferred_element_type=jnp.float32
    )
    largest = jnp.max(scores, axis=1, keepdims=True)
    weights = jnp.exp((scores - largest) * HEAD_DIM ** (-0.5))
    row_sums = jnp.sum(weights, axis=1, keepdims=True)
    mixed = jnp.dot(weights.astype(jnp.bfloat16), values, preferred_element_type=jnp.float32)
    return mixed / row_sums


def columns_of(index):
    return pl.ds(pl.multiple_of(index * HEAD_DIM, HEAD_DIM), HEAD_DIM)


def kernel(
    views,
    head_parts,
    ray_ref,
    up_ref,
    down_ref,
    key_ref,
    value_ref,
    query_ref,
    video_key_ref,
    video_value_ref,
    cross_query_ref,
    own_ref,
    cross_out_ref,
    up_full,
    down_full,
    key_full,
    value_full,
    cross_queries,
    ray_tokens,
    hidden_ref,
    partials_out,
    partials_in,
    rays,
    query_heads,
    pair_heads,
    own_heads,
    cross_ref,
    weight_local,
    weight_send,
    weight_recv,
    query_recv,
    pair_recv,
    relay_recv,
    bulk_send,
    relay_send,
    partial_send,
    partial_recv,
    ray_send,
    ray_recv,
    share_send,
    share_recv,
    pair_ray_send,
    pair_ray_recv,
    own_send,
    own_recv,
    own_local,
    cross_sem,
    view_greeted,
    part_greeted,
    core_greeted,
):
    view = lax.axis_index("view")
    part = lax.axis_index("head")
    core = lax.axis_index("dp")
    other = 1 - core
    rows = query_ref.shape[0]
    head_count = query_ref.shape[1] // HEAD_DIM
    per_view = head_count // views
    ray_rows = ray_ref.shape[0]
    half = up_ref.shape[0]
    inner = up_ref.shape[1]
    share = ray_ref.shape[1] // head_parts
    side = views // 2

    peers = [lax.rem(view + step, views) for step in range(1, views)]
    part_peers = [lax.rem(part + step, head_parts) for step in range(1, head_parts)]

    ordered_peers = [jnp.where(step < view, view - 1 - step, step + 1) for step in range(views - 1)]

    barrier = pltpu.get_barrier_semaphore()

    def enter(axis, peer, first):
        @pl.when(first)
        def _():
            pl.semaphore_signal(barrier, inc=1, device_id={axis: peer}, device_id_type=MESH)

    def answer(axis, peer, position, greeted, second):
        @pl.when(second)
        def _():
            pl.semaphore_signal(
                greeted.at[position], inc=1, device_id={axis: peer}, device_id_type=MESH
            )

    for peer in part_peers:
        enter("head", peer, part < peer)
    enter("dp", other, core == 1)
    for peer in ordered_peers:
        enter("view", peer, view < peer)
    earlier = view + part + other

    @pl.when(earlier > 0)
    def _():
        pl.semaphore_wait(barrier, earlier)

    for peer in ordered_peers:
        answer("view", peer, view, view_greeted, view > peer)
    for peer in part_peers:
        answer("head", peer, part, part_greeted, part > peer)
    answer("dp", other, core, core_greeted, core == 0)

    depth = pl.ds(pl.multiple_of(core * half, half), half)
    weight_pairs = (
        (up_ref, up_full.at[core]),
        (down_ref, down_full.at[core]),
        (key_ref, key_full.at[depth]),
        (value_ref, value_full.at[depth]),
    )
    local_copies = [
        pltpu.make_async_copy(source, slot, weight_local.at[index])
        for index, (source, slot) in enumerate(weight_pairs)
    ]
    local_copies.append(
        pltpu.make_async_copy(cross_query_ref, cross_queries, weight_local.at[4])
    )
    remote_copies = [
        pltpu.make_async_remote_copy(
            src_ref=source,
            dst_ref=slot,
            send_sem=weight_send.at[index],
            recv_sem=weight_recv.at[index],
            device_id={"dp": other},
            device_id_type=MESH,
        )
        for index, (source, slot) in enumerate(weight_pairs)
    ]
    local_copies.append(pltpu.make_async_copy(ray_ref, ray_tokens, weight_local.at[5]))
    own_rows = pl.ds(pl.multiple_of(view * rows, rows), rows)

    def keep_heads(index, carry):
        columns = columns_of(view * per_view + index)
        pltpu.make_async_copy(
            query_ref.at[:, columns], query_heads.at[index, own_rows], query_recv.at[index]
        ).start()
        pltpu.make_async_copy(
            video_key_ref.at[:, columns],
            pair_heads.at[index, core, 0, own_rows],
            pair_recv.at[index],
        ).start()
        pltpu.make_async_copy(
            video_value_ref.at[:, columns],
            pair_heads.at[index, core, 1, own_rows],
            pair_recv.at[index],
        ).start()
        return carry


    def send_head(index, peer):
        columns = columns_of(peer * per_view + index)
        for tensor, (source, target, arrived) in enumerate((
            (video_key_ref, pair_heads.at[index, core, 0, own_rows], pair_recv.at[index]),
            (video_value_ref, pair_heads.at[index, core, 1, own_rows], pair_recv.at[index]),
            (query_ref, query_heads.at[index, own_rows], query_recv.at[index]),
        )):
            pltpu.make_async_remote_copy(
                src_ref=source.at[:, columns],
                dst_ref=target,
                send_sem=bulk_send.at[tensor],
                recv_sem=arrived,
                device_id={"view": peer},
                device_id_type=MESH,
            ).start()

    def send_heads(index, carry):
        for peer in peers:
            send_head(index, peer)
        return carry

    def send_far(index, carry):
        for peer in peers:
            @pl.when(peer // side != view // side)
            def _():
                send_head(index, peer)
        return carry

    def send_near(index, carry):
        for peer in peers:
            @pl.when(peer // side == view // side)
            def _():
                send_head(index, peer)
        return carry

    first_heads = min(FIRST_HEADS, per_view)
    for step, peer in enumerate(ordered_peers):
        @pl.when(step >= view)
        def _():
            pl.semaphore_wait(view_greeted.at[step + 1], 1)

        def send_first(index, carry):
            send_head(index, peer)
            return carry

        lax.fori_loop(0, first_heads, send_first, 0)

    @pl.when(core == 1)
    def _():
        pl.semaphore_wait(core_greeted.at[0], 1)

    for copy in remote_copies[:2]:
        copy.start()
    for copy in local_copies[::-1]:
        copy.start()
    lax.fori_loop(0, per_view, keep_heads, 0)
    for copy in remote_copies[2:]:
        copy.start()

    local_copies[5].wait()
    tokens = ray_tokens[...]
    normed = rms_normed(tokens).astype(jnp.bfloat16)
    local_copies[0].wait()
    remote_copies[0].wait_recv()
    tile = min(512, inner)

    def up_tile(index, carry):
        columns = pl.ds(pl.multiple_of(index * tile, tile), tile)
        total = jnp.dot(normed[:, :half], up_full[0, :, columns], preferred_element_type=jnp.float32)
        total += jnp.dot(normed[:, half:], up_full[1, :, columns], preferred_element_type=jnp.float32)
        hidden_ref[:, columns] = jax.nn.gelu(total).astype(jnp.bfloat16)
        return carry

    lax.fori_loop(0, inner // tile, up_tile, 0)
    local_copies[1].wait()
    remote_copies[1].wait_recv()
    branch = jnp.concatenate(
        [
            lax.dot_general(
                hidden_ref[...],
                down_full[index],
                (((1,), (1,)), ((), ())),
                preferred_element_type=jnp.float32,
            )
            for index in range(2)
        ],
        axis=1,
    )
    for index in range(head_parts):
        partials_out[index] = branch[:, index * share : (index + 1) * share]
    partial_copies = [
        pltpu.make_async_remote_copy(
            src_ref=partials_out.at[peer],
            dst_ref=partials_in.at[step],
            send_sem=partial_send.at[step],
            recv_sem=partial_recv.at[step],
            device_id={"head": peer},
            device_id_type=MESH,
        )
        for step, peer in enumerate(part_peers)
    ]
    for later in range(1, head_parts):
        @pl.when(part < later)
        def _():
            pl.semaphore_wait(part_greeted.at[later], 1)

    for copy in partial_copies:
        copy.start()
    for copy in partial_copies:
        copy.wait_recv()
    total_share = partials_out[part]
    for index in range(head_parts - 1):
        total_share += partials_in[index]
    share_columns = pl.ds(pl.multiple_of(part * share, share), share)
    rays[core, part, view] = (
        ray_tokens[:, share_columns].astype(jnp.float32) + total_share
    ).astype(jnp.bfloat16)
    side_start = (view // side) * side
    far_start = side - side_start
    gate = jnp.where(side_start == 0, side - 1, side)
    far_gate = 2 * side - 1 - gate
    side_peers = [side_start + lax.rem(view - side_start + step, side) for step in range(1, side)]

    def ray_copy(source, peer, index, arrived):
        return pltpu.make_async_remote_copy(
            src_ref=source,
            dst_ref=source,
            send_sem=ray_send.at[index],
            recv_sem=ray_recv.at[arrived],
            device_id={"view": peer},
            device_id_type=MESH,
        )

    mine = rays.at[core, part, view]
    far_slots = rays.at[core, part, pl.ds(far_start, side)]
    ray_copies = [ray_copy(mine, peer, step, step) for step, peer in enumerate(side_peers)]
    far_copy = ray_copy(mine, far_gate, side - 1, side - 1)
    far_copy.start()
    for copy in ray_copies:
        copy.start()
    second_heads = min(first_heads + SECOND_HEADS, per_view)
    facing_view = jnp.logical_or(view == side - 1, view == side)

    @pl.when(facing_view)
    def _():
        lax.fori_loop(first_heads, second_heads, send_heads, 0)
        lax.fori_loop(second_heads, per_view, send_far, 0)


    def relay(index):
        return pltpu.make_async_remote_copy(
            src_ref=pair_heads.at[index, core],
            dst_ref=pair_heads.at[index, core],
            send_sem=relay_send.at[index],
            recv_sem=relay_recv.at[index],
            device_id={"dp": other},
            device_id_type=MESH,
        )

    def pass_on(index, carry):
        arrived = pair_heads.at[index, core]
        pltpu.make_async_copy(arrived, arrived, pair_recv.at[index]).wait()
        relay(index).start()
        return carry

    last_view = far_start + side - 1

    def own_copy(index, peer):
        return pltpu.make_async_remote_copy(
            src_ref=own_heads.at[index, pl.ds(pl.multiple_of(peer * rows, rows), rows)],
            dst_ref=own_ref.at[:, columns_of(view * per_view + index)],
            send_sem=own_send,
            recv_sem=own_recv,
            device_id={"view": peer},
            device_id_type=MESH,
        )

    def send_last(index, carry):
        own_copy(index, last_view).start()
        return carry

    holds = jnp.logical_not(facing_view)

    def not_last(index, peer):
        return jnp.logical_or(index < NOT_DEFERRED, peer != last_view)

    def attend(index, carry):
        arrived = query_heads.at[index]
        pltpu.make_async_copy(arrived, arrived, query_recv.at[index]).wait()
        relay(index).wait_recv()
        keys = pair_heads[index, :, 0].reshape(2 * views * rows, HEAD_DIM)
        values = pair_heads[index, :, 1].reshape(2 * views * rows, HEAD_DIM)
        block = min(QUERY_BLOCK, views * rows)

        def attend_block(piece, inner_carry):
            span = pl.ds(pl.multiple_of(piece * block, block), block)
            own_heads[index, span] = softmax_mix(query_heads[index, span], keys, values).astype(
                jnp.bfloat16
            )
            return inner_carry

        lax.fori_loop(0, views * rows // block, attend_block, 0)
        columns = columns_of(view * per_view + index)
        pltpu.make_async_copy(
            own_heads.at[index, own_rows], own_ref.at[:, columns], own_local
        ).start()
        for peer in peers:
            held = jnp.logical_and(
                jnp.logical_and(holds, index < second_heads), peer // side != view // side
            )

            @pl.when(jnp.logical_and(not_last(index, peer), jnp.logical_not(held)))
            def _():
                own_copy(index, peer).start()

        return carry

    def send_held(index, carry):
        for peer in peers:
            far = peer // side != view // side

            @pl.when(jnp.logical_and(not_last(index, peer), far))
            def _():
                own_copy(index, peer).start()

        return carry

    lax.fori_loop(0, 1, pass_on, 0)

    @pl.when(jnp.logical_not(facing_view))
    def _():
        lax.fori_loop(first_heads, second_heads, send_heads, 0)

    lax.fori_loop(1, first_heads, pass_on, 0)
    pltpu.make_async_copy(far_slots, far_slots, ray_recv.at[side - 1]).wait()
    gate_copies = [
        ray_copy(far_slots, peer, side + step, side - 1) for step, peer in enumerate(side_peers)
    ]

    @pl.when(view == gate)
    def _():
        for copy in gate_copies:
            copy.start()


    @pl.when(facing_view)
    def _():
        lax.fori_loop(second_heads, per_view, send_near, 0)
        lax.fori_loop(per_view, per_view, send_heads, 0)

    @pl.when(jnp.logical_not(facing_view))
    def _():
        lax.fori_loop(second_heads, per_view, send_heads, 0)

    for copy in ray_copies:
        copy.wait_recv()
    share_copies = [
        pltpu.make_async_remote_copy(
            src_ref=rays.at[core, part],
            dst_ref=rays.at[core, part],
            send_sem=share_send.at[step],
            recv_sem=share_recv.at[step],
            device_id={"head": peer},
            device_id_type=MESH,
        )
        for step, peer in enumerate(part_peers)
    ]
    for copy in share_copies:
        copy.start()
    lax.fori_loop(0, first_heads, attend, 0)
    lax.fori_loop(first_heads, second_heads, pass_on, 0)
    for copy in share_copies:
        copy.wait_recv()
    ray_relay = pltpu.make_async_remote_copy(
        src_ref=rays.at[core],
        dst_ref=rays.at[core],
        send_sem=pair_ray_send,
        recv_sem=pair_ray_recv,
        device_id={"dp": other},
        device_id_type=MESH,
    )
    ray_relay.start()
    lax.fori_loop(first_heads, second_heads, attend, 0)

    ray_relay.wait_recv()
    for index in (2, 3):
        local_copies[index].wait()
        remote_copies[index].wait_recv()
    local_copies[4].wait()
    ray_shares = [
        rays[:, index].reshape(2 * views * ray_rows, share) for index in range(head_parts)
    ]
    group = 2 if head_count % 2 == 0 else 1
    width = group * HEAD_DIM

    def cross_group(index, carry):
        columns = pl.ds(pl.multiple_of(index * width, width), width)

        def project(full):
            total = 0.0
            for index, ray_share in enumerate(ray_shares):
                total += jnp.dot(
                    ray_share,
                    full[index * share : (index + 1) * share, columns],
                    preferred_element_type=jnp.float32,
                )
            return total.astype(jnp.bfloat16)

        keys, values = project(key_full), project(value_full)
        queries = cross_queries[:, columns]
        results = []
        for lane in range(group):
            span = slice(lane * HEAD_DIM, (lane + 1) * HEAD_DIM)
            results.append(softmax_mix(queries[:, span], keys[:, span], values[:, span]))
        cross_ref[:, columns] = jnp.concatenate(results, axis=1)
        return carry

    lax.fori_loop(0, head_count // group, cross_group, 0)
    cross_copy = pltpu.make_async_copy(cross_ref, cross_out_ref, cross_sem)
    cross_copy.start()

    lax.fori_loop(second_heads, per_view, pass_on, 0)

    @pl.when(holds)
    def _():
        lax.fori_loop(0, second_heads, send_held, 0)

    last_head = max(second_heads, per_view - 1)
    sent_ahead = jnp.logical_and(jnp.logical_and(holds, view >= side), core == 1)
    middle = jnp.where(sent_ahead, min(SENT_AHEAD, per_view), NOT_DEFERRED)
    lax.fori_loop(second_heads, last_head, attend, 0)
    lax.fori_loop(NOT_DEFERRED, middle, send_last, 0)
    lax.fori_loop(last_head, per_view, attend, 0)
    lax.fori_loop(middle, per_view, send_last, 0)

    sent_copies = remote_copies + partial_copies + ray_copies + share_copies
    for copy in sent_copies + [far_copy, ray_relay]:
        copy.wait_send()

    @pl.when(view == gate)
    def _():
        for copy in gate_copies:
            copy.wait_send()

    def relay_sent(index, carry):
        relay(index).wait_send()
        return carry

    lax.fori_loop(0, per_view, relay_sent, 0)
    for tensor in range(3):
        sent = query_heads.at[:, pl.ds(0, (views - 1) * rows)]
        pltpu.make_async_copy(sent, sent, bulk_send.at[tensor]).wait()
    cross_copy.wait()
    kept = own_heads.at[:, pl.ds(0, rows)]
    pltpu.make_async_copy(kept, kept, own_local).wait()
    returned = own_heads.at[:, pl.ds(0, (views - 1) * rows)]
    pltpu.make_async_copy(returned, returned, own_send).wait()
    pltpu.make_async_copy(returned, returned, own_recv).wait()


def add_kernel(blocks, own_ref, cross_ref, out_ref, sums, sems):
    size = own_ref.shape[0] // blocks
    copies = []
    for index in range(blocks):
        span = pl.ds(index * size, size)
        sums[span] = (cross_ref[span] + own_ref[span].astype(jnp.float32)).astype(jnp.bfloat16)
        copies.append(pltpu.make_async_copy(sums.at[span], out_ref.at[span], sems.at[index]))
        copies[-1].start()
    for copy in copies:
        copy.wait()


def fused_body(views, head_parts, *args):
    ray_tokens, up_weight, down_weight, key_weight, value_weight, video_queries = args[:6]
    rows, columns = video_queries.shape
    per_view = columns // HEAD_DIM // views
    ray_rows, ray_width = ray_tokens.shape
    half, inner = up_weight.shape
    share = ray_width // head_parts
    bf16, f32 = jnp.bfloat16, jnp.float32
    dma = pltpu.SemaphoreType.DMA
    anywhere = pl.BlockSpec(memory_space=pl.ANY)
    args = [pltpu.with_memory_space_constraint(arg, pltpu.HBM) for arg in args]
    own, cross = pl.pallas_call(
        functools.partial(kernel, views, head_parts),
        out_shape=(pltpu.VMEM((rows, columns), bf16), pltpu.VMEM((rows, columns), f32)),
        in_specs=[anywhere] * 9,
        out_specs=(anywhere, anywhere),
        scratch_shapes=[
            pltpu.VMEM((2,) + up_weight.shape, bf16),
            pltpu.VMEM((2,) + down_weight.shape, bf16),
            pltpu.VMEM((2 * half, columns), bf16),
            pltpu.VMEM((2 * half, columns), bf16),
            pltpu.VMEM((rows, columns), bf16),
            pltpu.VMEM((ray_rows, ray_width), bf16),
            pltpu.VMEM((ray_rows, inner), bf16),
            pltpu.VMEM((head_parts, ray_rows, share), f32),
            pltpu.VMEM((head_parts, ray_rows, share), f32),
            pltpu.VMEM((2, head_parts, views, ray_rows, share), bf16),
            pltpu.VMEM((per_view, views * rows, HEAD_DIM), bf16),
            pltpu.VMEM((per_view, 2, 2, views * rows, HEAD_DIM), bf16),
            pltpu.VMEM((per_view, views * rows, HEAD_DIM), bf16),
            pltpu.VMEM((rows, columns), f32),
            dma((6,)),
            dma((4,)),
            dma((4,)),
            dma((per_view,)),
            dma((per_view,)),
            dma((per_view,)),
            dma((3,)),
            dma((per_view,)),
            dma((max(head_parts - 1, 1),)),
            dma((max(head_parts - 1, 1),)),
            dma((views,)),
            dma((views,)),
            dma((max(head_parts - 1, 1),)),
            dma((max(head_parts - 1, 1),)),
            dma,
            dma,
            dma,
            dma,
            dma,
            dma,
            pltpu.SemaphoreType.REGULAR((views,)),
            pltpu.SemaphoreType.REGULAR((head_parts,)),
            pltpu.SemaphoreType.REGULAR((2,)),
        ],
        compiler_params=pltpu.CompilerParams(
            collective_id=0, has_side_effects=True, vmem_limit_bytes=48 * 2**20
        ),
    )(*args)
    vmem = pl.BlockSpec(memory_space=pltpu.VMEM)
    blocks = ADD_BLOCKS if rows % (16 * ADD_BLOCKS) == 0 else 1
    return pl.pallas_call(
        functools.partial(add_kernel, blocks),
        out_shape=jax.ShapeDtypeStruct((rows, columns), bf16),
        in_specs=[vmem, vmem],
        out_specs=anywhere,
        scratch_shapes=[pltpu.VMEM((rows, columns), bf16), dma((blocks,))],
        compiler_params=pltpu.CompilerParams(vmem_limit_bytes=8 * 2**20),
    )(
        pltpu.with_memory_space_constraint(own, pltpu.VMEM),
        pltpu.with_memory_space_constraint(cross, pltpu.VMEM),
    )


def solution(mesh):
    views, head_parts = mesh.shape["view"], mesh.shape["head"]

    def routed(*args):
        head_count = args[5].shape[1] // HEAD_DIM
        if (
            mesh.shape["dp"] == 2
            and views % 2 == 0
            and head_count % views == 0
            and args[0].shape[1] % (head_parts * HEAD_DIM) == 0
        ):
            return fused_body(views, head_parts, *args)
        return body(*args)

    in_specs = (
        P(("groups", "view", "dp"), None),
        P("dp", "head"),
        P("dp", "head"),
        P("dp", "head"),
        P("dp", "head"),
        P(("groups", "view", "dp"), "head"),
        P(("groups", "view", "dp"), "head"),
        P(("groups", "view", "dp"), "head"),
        P(("groups", "view", "dp"), "head"),
    )
    out_specs = P(("groups", "view", "dp"), "head")
    return jax.shard_map(routed, mesh=mesh, in_specs=in_specs, out_specs=out_specs, check_vma=False)
```

```python
import functools

import jax
import jax.numpy as jnp
from jax import lax
from jax.experimental import pallas as pl
from jax.experimental.pallas import tpu as pltpu
from jax.sharding import PartitionSpec as P

HEAD_DIM = 128


epsilon = 1e-06


def rms_normed(values_in):
    widened = values_in.astype(jnp.float32)
    mean_square = jnp.mean(widened * widened, axis=1, keepdims=True)
    return widened * lax.rsqrt(mean_square + epsilon)


def empty_state(head_count, row_count):
    running_max = jnp.full((head_count, row_count), -1e30, jnp.float32)
    running_sum = jnp.zeros((head_count, row_count), jnp.float32)
    weighted = jnp.zeros((head_count, row_count, HEAD_DIM), jnp.float32)
    return (running_max, running_sum, weighted)


def absorb(state_now, query_head_rows, key_piece, value_piece):
    running_max, running_sum, weighted = state_now
    head_count = query_head_rows.shape[1]
    key_head_rows = key_piece.reshape(key_piece.shape[0], head_count, HEAD_DIM)
    value_head_rows = value_piece.reshape(value_piece.shape[0], head_count, HEAD_DIM)
    scores = jnp.einsum(
        "xrz,frz->rxf", query_head_rows, key_head_rows, preferred_element_type=jnp.float32
    ) * HEAD_DIM ** (-0.5)
    new_max = jnp.maximum(running_max, jnp.max(scores, axis=2))
    exponent = jnp.exp(scores - new_max[:, :, None])
    running_sum = jnp.sum(exponent, axis=2)
    weighted = jnp.einsum(
        "bau,uby->bay",
        exponent.astype(jnp.bfloat16),
        value_head_rows,
        preferred_element_type=jnp.float32,
    )
    return (new_max, running_sum, weighted)


def finish(state_now):
    running_max, running_sum, weighted = state_now
    result = weighted / running_sum[:, :, None]
    head_count, row_count = running_sum.shape
    return result.transpose(1, 0, 2).reshape(row_count, head_count * HEAD_DIM)


def body(
    ray_tokens,
    up_weight,
    down_weight,
    key_weight,
    value_weight,
    video_queries,
    video_keys,
    video_values,
    cross_queries,
):
    row_count = video_queries.shape[0]
    head_count = video_queries.shape[1] // HEAD_DIM
    up_full, down_full, key_full, value_full = (
        lax.all_gather(up_weight, "dp", axis=0, tiled=True),
        lax.all_gather(down_weight, "dp", axis=0, tiled=True),
        lax.all_gather(key_weight, "dp", axis=0, tiled=True),
        lax.all_gather(value_weight, "dp", axis=0, tiled=True),
    )
    normed = rms_normed(ray_tokens).astype(jnp.bfloat16)
    hidden = jax.nn.gelu(jnp.dot(normed, up_full, preferred_element_type=jnp.float32)).astype(
        jnp.bfloat16
    )
    partial_branch = lax.dot_general(
        hidden, down_full, (((1,), (1,)), ((), ())), preferred_element_type=jnp.float32
    )
    branch = lax.psum(partial_branch, "head")
    rays = (ray_tokens.astype(jnp.float32) + branch).astype(jnp.bfloat16)
    cross_heads = cross_queries.reshape(row_count, head_count, HEAD_DIM)
    piece = lax.all_gather(rays, ("view", "dp"), axis=0, tiled=True)
    piece_keys = jnp.dot(piece, key_full, preferred_element_type=jnp.float32).astype(jnp.bfloat16)
    piece_values = jnp.dot(piece, value_full, preferred_element_type=jnp.float32).astype(
        jnp.bfloat16
    )
    cross_state = absorb(empty_state(head_count, row_count), cross_heads, piece_keys, piece_values)
    cross = finish(cross_state)
    local_head_group = video_queries.reshape(row_count, head_count, HEAD_DIM)
    own_state = absorb(
        empty_state(head_count, row_count),
        local_head_group,
        lax.all_gather(video_keys, ("view", "dp"), axis=0, tiled=True),
        lax.all_gather(video_values, ("view", "dp"), axis=0, tiled=True),
    )
    own = finish(own_state)
    return (own + cross).astype(jnp.bfloat16)


MESH = pl.DeviceIdType.MESH
QUERY_BLOCK = 256
FIRST_HEADS = 2
SECOND_HEADS = 1
NOT_DEFERRED = 1
SENT_AHEAD = 2
ADD_BLOCKS = 8


def softmax_mix(queries, keys, values):
    scores = lax.dot_general(
        queries, keys, (((1,), (1,)), ((), ())), preferred_element_type=jnp.float32
    )
    largest = jnp.max(scores, axis=1, keepdims=True)
    weights = jnp.exp((scores - largest) * HEAD_DIM ** (-0.5))
    row_sums = jnp.sum(weights, axis=1, keepdims=True)
    mixed = jnp.dot(weights.astype(jnp.bfloat16), values, preferred_element_type=jnp.float32)
    return mixed / row_sums


def columns_of(index):
    return pl.ds(pl.multiple_of(index * HEAD_DIM, HEAD_DIM), HEAD_DIM)


def kernel(
    views,
    head_parts,
    ray_ref,
    up_ref,
    down_ref,
    key_ref,
    value_ref,
    query_ref,
    video_key_ref,
    video_value_ref,
    cross_query_ref,
    own_ref,
    cross_out_ref,
    up_full,
    down_full,
    key_full,
    value_full,
    cross_queries,
    ray_tokens,
    hidden_ref,
    partials_out,
    partials_in,
    rays,
    query_heads,
    pair_heads,
    own_heads,
    detour_ref,
    cross_ref,
    weight_local,
    weight_send,
    weight_recv,
    query_recv,
    pair_recv,
    relay_recv,
    bulk_send,
    relay_send,
    partial_send,
    partial_recv,
    ray_send,
    ray_recv,
    share_send,
    share_recv,
    pair_ray_send,
    pair_ray_recv,
    own_send,
    own_recv,
    own_local,
    cross_sem,
    detour_send,
    detour_recv,
    view_greeted,
    part_greeted,
    core_greeted,
):
    view = lax.axis_index("view")
    part = lax.axis_index("head")
    core = lax.axis_index("dp")
    other = 1 - core
    rows = query_ref.shape[0]
    head_count = query_ref.shape[1] // HEAD_DIM
    per_view = head_count // views
    ray_rows = ray_ref.shape[0]
    half = up_ref.shape[0]
    inner = up_ref.shape[1]
    share = ray_ref.shape[1] // head_parts
    side = views // 2

    peers = [lax.rem(view + step, views) for step in range(1, views)]
    part_peers = [lax.rem(part + step, head_parts) for step in range(1, head_parts)]

    ordered_peers = [jnp.where(step < view, view - 1 - step, step + 1) for step in range(views - 1)]

    barrier = pltpu.get_barrier_semaphore()

    def enter(axis, peer, first):
        @pl.when(first)
        def _():
            pl.semaphore_signal(barrier, inc=1, device_id={axis: peer}, device_id_type=MESH)

    def answer(axis, peer, position, greeted, second):
        @pl.when(second)
        def _():
            pl.semaphore_signal(
                greeted.at[position], inc=1, device_id={axis: peer}, device_id_type=MESH
            )

    for peer in part_peers:
        enter("head", peer, part < peer)
    enter("dp", other, core == 1)
    for peer in ordered_peers:
        enter("view", peer, view < peer)
    earlier = view + part + other

    @pl.when(earlier > 0)
    def _():
        pl.semaphore_wait(barrier, earlier)

    for peer in ordered_peers:
        answer("view", peer, view, view_greeted, view > peer)
    for peer in part_peers:
        answer("head", peer, part, part_greeted, part > peer)
    answer("dp", other, core, core_greeted, core == 0)

    depth = pl.ds(pl.multiple_of(core * half, half), half)
    weight_pairs = (
        (up_ref, up_full.at[core]),
        (down_ref, down_full.at[core]),
        (key_ref, key_full.at[depth]),
        (value_ref, value_full.at[depth]),
    )
    local_copies = [
        pltpu.make_async_copy(source, slot, weight_local.at[index])
        for index, (source, slot) in enumerate(weight_pairs)
    ]
    local_copies.append(
        pltpu.make_async_copy(cross_query_ref, cross_queries, weight_local.at[4])
    )
    remote_copies = [
        pltpu.make_async_remote_copy(
            src_ref=source,
            dst_ref=slot,
            send_sem=weight_send.at[index],
            recv_sem=weight_recv.at[index],
            device_id={"dp": other},
            device_id_type=MESH,
        )
        for index, (source, slot) in enumerate(weight_pairs)
    ]
    local_copies.append(pltpu.make_async_copy(ray_ref, ray_tokens, weight_local.at[5]))
    own_rows = pl.ds(pl.multiple_of(view * rows, rows), rows)

    def keep_heads(index, carry):
        columns = columns_of(view * per_view + index)
        pltpu.make_async_copy(
            query_ref.at[:, columns], query_heads.at[index, own_rows], query_recv.at[index]
        ).start()
        pltpu.make_async_copy(
            video_key_ref.at[:, columns],
            pair_heads.at[index, core, 0, own_rows],
            pair_recv.at[index],
        ).start()
        pltpu.make_async_copy(
            video_value_ref.at[:, columns],
            pair_heads.at[index, core, 1, own_rows],
            pair_recv.at[index],
        ).start()
        return carry


    def send_head(index, peer):
        columns = columns_of(peer * per_view + index)
        for tensor, (source, target, arrived) in enumerate((
            (video_key_ref, pair_heads.at[index, core, 0, own_rows], pair_recv.at[index]),
            (video_value_ref, pair_heads.at[index, core, 1, own_rows], pair_recv.at[index]),
            (query_ref, query_heads.at[index, own_rows], query_recv.at[index]),
        )):
            pltpu.make_async_remote_copy(
                src_ref=source.at[:, columns],
                dst_ref=target,
                send_sem=bulk_send.at[tensor],
                recv_sem=arrived,
                device_id={"view": peer},
                device_id_type=MESH,
            ).start()

    def send_heads(index, carry):
        for peer in peers:
            send_head(index, peer)
        return carry

    def send_far(index, carry):
        for peer in peers:
            @pl.when(peer // side != view // side)
            def _():
                send_head(index, peer)
        return carry

    def send_near(index, carry):
        for peer in peers:
            @pl.when(peer // side == view // side)
            def _():
                send_head(index, peer)
        return carry

    first_heads = min(FIRST_HEADS, per_view)
    for step, peer in enumerate(ordered_peers):
        @pl.when(step >= view)
        def _():
            pl.semaphore_wait(view_greeted.at[step + 1], 1)

        def send_first(index, carry):
            send_head(index, peer)
            return carry

        lax.fori_loop(0, first_heads, send_first, 0)

    @pl.when(core == 1)
    def _():
        pl.semaphore_wait(core_greeted.at[0], 1)

    for copy in remote_copies[:2]:
        copy.start()
    for copy in local_copies[::-1]:
        copy.start()
    lax.fori_loop(0, per_view, keep_heads, 0)
    for copy in remote_copies[2:]:
        copy.start()

    local_copies[5].wait()
    tokens = ray_tokens[...]
    normed = rms_normed(tokens).astype(jnp.bfloat16)
    local_copies[0].wait()
    remote_copies[0].wait_recv()
    tile = min(512, inner)

    def up_tile(index, carry):
        columns = pl.ds(pl.multiple_of(index * tile, tile), tile)
        total = jnp.dot(normed[:, :half], up_full[0, :, columns], preferred_element_type=jnp.float32)
        total += jnp.dot(normed[:, half:], up_full[1, :, columns], preferred_element_type=jnp.float32)
        hidden_ref[:, columns] = jax.nn.gelu(total).astype(jnp.bfloat16)
        return carry

    lax.fori_loop(0, inner // tile, up_tile, 0)
    local_copies[1].wait()
    remote_copies[1].wait_recv()
    branch = jnp.concatenate(
        [
            lax.dot_general(
                hidden_ref[...],
                down_full[index],
                (((1,), (1,)), ((), ())),
                preferred_element_type=jnp.float32,
            )
            for index in range(2)
        ],
        axis=1,
    )
    for index in range(head_parts):
        partials_out[index] = branch[:, index * share : (index + 1) * share]
    partial_copies = [
        pltpu.make_async_remote_copy(
            src_ref=partials_out.at[peer],
            dst_ref=partials_in.at[step],
            send_sem=partial_send.at[step],
            recv_sem=partial_recv.at[step],
            device_id={"head": peer},
            device_id_type=MESH,
        )
        for step, peer in enumerate(part_peers)
    ]
    for later in range(1, head_parts):
        @pl.when(part < later)
        def _():
            pl.semaphore_wait(part_greeted.at[later], 1)

    for copy in partial_copies:
        copy.start()
    for copy in partial_copies:
        copy.wait_recv()
    total_share = partials_out[part]
    for index in range(head_parts - 1):
        total_share += partials_in[index]
    share_columns = pl.ds(pl.multiple_of(part * share, share), share)
    rays[core, part, view] = (
        ray_tokens[:, share_columns].astype(jnp.float32) + total_share
    ).astype(jnp.bfloat16)
    side_start = (view // side) * side
    far_start = side - side_start
    gate = jnp.where(side_start == 0, side - 1, side)
    far_gate = 2 * side - 1 - gate
    side_peers = [side_start + lax.rem(view - side_start + step, side) for step in range(1, side)]

    def ray_copy(source, peer, index, arrived):
        return pltpu.make_async_remote_copy(
            src_ref=source,
            dst_ref=source,
            send_sem=ray_send.at[index],
            recv_sem=ray_recv.at[arrived],
            device_id={"view": peer},
            device_id_type=MESH,
        )

    mine = rays.at[core, part, view]
    far_slots = rays.at[core, part, pl.ds(far_start, side)]
    ray_copies = [ray_copy(mine, peer, step, step) for step, peer in enumerate(side_peers)]
    far_copy = ray_copy(mine, far_gate, side - 1, side - 1)
    far_copy.start()
    for copy in ray_copies:
        copy.start()
    second_heads = min(first_heads + SECOND_HEADS, per_view)
    facing_view = jnp.logical_or(view == side - 1, view == side)

    @pl.when(facing_view)
    def _():
        lax.fori_loop(first_heads, second_heads, send_heads, 0)
        lax.fori_loop(second_heads, per_view, send_far, 0)


    def relay(index):
        return pltpu.make_async_remote_copy(
            src_ref=pair_heads.at[index, core],
            dst_ref=pair_heads.at[index, core],
            send_sem=relay_send.at[index],
            recv_sem=relay_recv.at[index],
            device_id={"dp": other},
            device_id_type=MESH,
        )

    def pass_on(index, carry):
        arrived = pair_heads.at[index, core]
        pltpu.make_async_copy(arrived, arrived, pair_recv.at[index]).wait()
        relay(index).start()
        return carry

    last_view = far_start + side - 1

    def own_copy(index, peer):
        return pltpu.make_async_remote_copy(
            src_ref=own_heads.at[index, pl.ds(pl.multiple_of(peer * rows, rows), rows)],
            dst_ref=own_ref.at[:, columns_of(view * per_view + index)],
            send_sem=own_send,
            recv_sem=own_recv,
            device_id={"view": peer},
            device_id_type=MESH,
        )

    gives = jnp.logical_and(facing_view, core == 0)
    takes = jnp.logical_and(facing_view, core == 1)
    detour_in = pltpu.make_async_remote_copy(
        src_ref=own_heads.at[per_view - 1, pl.ds(pl.multiple_of(last_view * rows, rows), rows)],
        dst_ref=detour_ref,
        send_sem=detour_send.at[0],
        recv_sem=detour_recv,
        device_id={"dp": other},
        device_id_type=MESH,
    )
    detour_out = pltpu.make_async_remote_copy(
        src_ref=detour_ref,
        dst_ref=own_ref.at[:, columns_of(view * per_view + per_view - 1)],
        send_sem=detour_send.at[1],
        recv_sem=own_recv,
        device_id={"view": last_view, "dp": other},
        device_id_type=MESH,
    )

    def send_last(index, carry):
        own_copy(index, last_view).start()
        return carry

    holds = jnp.logical_not(facing_view)

    def not_last(index, peer):
        return jnp.logical_or(index < NOT_DEFERRED, peer != last_view)

    def attend(index, carry):
        arrived = query_heads.at[index]
        pltpu.make_async_copy(arrived, arrived, query_recv.at[index]).wait()
        relay(index).wait_recv()
        keys = pair_heads[index, :, 0].reshape(2 * views * rows, HEAD_DIM)
        values = pair_heads[index, :, 1].reshape(2 * views * rows, HEAD_DIM)
        block = min(QUERY_BLOCK, views * rows)

        def attend_block(piece, inner_carry):
            span = pl.ds(pl.multiple_of(piece * block, block), block)
            own_heads[index, span] = softmax_mix(query_heads[index, span], keys, values).astype(
                jnp.bfloat16
            )
            return inner_carry

        lax.fori_loop(0, views * rows // block, attend_block, 0)
        columns = columns_of(view * per_view + index)
        pltpu.make_async_copy(
            own_heads.at[index, own_rows], own_ref.at[:, columns], own_local
        ).start()
        for peer in peers:
            held = jnp.logical_and(
                jnp.logical_and(holds, index < second_heads), peer // side != view // side
            )

            @pl.when(jnp.logical_and(not_last(index, peer), jnp.logical_not(held)))
            def _():
                own_copy(index, peer).start()

        return carry

    def send_held(index, carry):
        for peer in peers:
            far = peer // side != view // side

            @pl.when(jnp.logical_and(not_last(index, peer), far))
            def _():
                own_copy(index, peer).start()

        return carry

    lax.fori_loop(0, 1, pass_on, 0)

    @pl.when(jnp.logical_not(facing_view))
    def _():
        lax.fori_loop(first_heads, second_heads, send_heads, 0)

    lax.fori_loop(1, first_heads, pass_on, 0)
    pltpu.make_async_copy(far_slots, far_slots, ray_recv.at[side - 1]).wait()
    gate_copies = [
        ray_copy(far_slots, peer, side + step, side - 1) for step, peer in enumerate(side_peers)
    ]

    @pl.when(view == gate)
    def _():
        for copy in gate_copies:
            copy.start()


    @pl.when(facing_view)
    def _():
        lax.fori_loop(second_heads, per_view, send_near, 0)
        lax.fori_loop(per_view, per_view, send_heads, 0)

    @pl.when(jnp.logical_not(facing_view))
    def _():
        lax.fori_loop(second_heads, per_view, send_heads, 0)

    for copy in ray_copies:
        copy.wait_recv()
    share_copies = [
        pltpu.make_async_remote_copy(
            src_ref=rays.at[core, part],
            dst_ref=rays.at[core, part],
            send_sem=share_send.at[step],
            recv_sem=share_recv.at[step],
            device_id={"head": peer},
            device_id_type=MESH,
        )
        for step, peer in enumerate(part_peers)
    ]
    for copy in share_copies:
        copy.start()
    lax.fori_loop(0, first_heads, attend, 0)
    lax.fori_loop(first_heads, second_heads, pass_on, 0)
    for copy in share_copies:
        copy.wait_recv()
    ray_relay = pltpu.make_async_remote_copy(
        src_ref=rays.at[core],
        dst_ref=rays.at[core],
        send_sem=pair_ray_send,
        recv_sem=pair_ray_recv,
        device_id={"dp": other},
        device_id_type=MESH,
    )
    ray_relay.start()
    lax.fori_loop(first_heads, second_heads, attend, 0)

    ray_relay.wait_recv()
    for index in (2, 3):
        local_copies[index].wait()
        remote_copies[index].wait_recv()
    local_copies[4].wait()
    ray_shares = [
        rays[:, index].reshape(2 * views * ray_rows, share) for index in range(head_parts)
    ]
    group = 2 if head_count % 2 == 0 else 1
    width = group * HEAD_DIM

    def cross_group(index, carry):
        columns = pl.ds(pl.multiple_of(index * width, width), width)

        def project(full):
            total = 0.0
            for index, ray_share in enumerate(ray_shares):
                total += jnp.dot(
                    ray_share,
                    full[index * share : (index + 1) * share, columns],
                    preferred_element_type=jnp.float32,
                )
            return total.astype(jnp.bfloat16)

        keys, values = project(key_full), project(value_full)
        queries = cross_queries[:, columns]
        results = []
        for lane in range(group):
            span = slice(lane * HEAD_DIM, (lane + 1) * HEAD_DIM)
            results.append(softmax_mix(queries[:, span], keys[:, span], values[:, span]))
        cross_ref[:, columns] = jnp.concatenate(results, axis=1)
        return carry

    lax.fori_loop(0, head_count // group, cross_group, 0)
    cross_copy = pltpu.make_async_copy(cross_ref, cross_out_ref, cross_sem)
    cross_copy.start()

    lax.fori_loop(second_heads, per_view, pass_on, 0)

    @pl.when(holds)
    def _():
        lax.fori_loop(0, second_heads, send_held, 0)

    last_head = max(second_heads, per_view - 1)
    sent_ahead = jnp.logical_and(jnp.logical_and(holds, view >= side), core == 1)
    middle = jnp.where(sent_ahead, min(SENT_AHEAD, per_view), NOT_DEFERRED)
    lax.fori_loop(second_heads, last_head, attend, 0)
    lax.fori_loop(NOT_DEFERRED, middle, send_last, 0)
    lax.fori_loop(last_head, per_view, attend, 0)

    @pl.when(gives)
    def _():
        detour_in.start()

    @pl.when(takes)
    def _():
        detour_in.wait_recv()
        detour_out.start()

    lax.fori_loop(middle, jnp.where(gives, per_view - 1, per_view), send_last, 0)

    sent_copies = remote_copies + partial_copies + ray_copies + share_copies
    for copy in sent_copies + [far_copy, ray_relay]:
        copy.wait_send()

    @pl.when(view == gate)
    def _():
        for copy in gate_copies:
            copy.wait_send()

    def relay_sent(index, carry):
        relay(index).wait_send()
        return carry

    lax.fori_loop(0, per_view, relay_sent, 0)
    for tensor in range(3):
        sent = query_heads.at[:, pl.ds(0, (views - 1) * rows)]
        pltpu.make_async_copy(sent, sent, bulk_send.at[tensor]).wait()
    cross_copy.wait()
    kept = own_heads.at[:, pl.ds(0, rows)]
    pltpu.make_async_copy(kept, kept, own_local).wait()
    returned = own_heads.at[:, pl.ds(0, (views - 1) * rows)]
    direct = own_heads.at[pl.ds(0, per_view - 1), pl.ds(0, (views - 1) * rows)]
    pltpu.make_async_copy(direct, direct, own_send).wait()
    direct = own_heads.at[0, pl.ds(0, (views - 2) * rows)]
    pltpu.make_async_copy(direct, direct, own_send).wait()

    @pl.when(gives)
    def _():
        detour_in.wait_send()

    @pl.when(jnp.logical_not(gives))
    def _():
        single = own_heads.at[0, pl.ds(0, rows)]
        pltpu.make_async_copy(single, single, own_send).wait()

    @pl.when(takes)
    def _():
        detour_out.wait_send()

    pltpu.make_async_copy(returned, returned, own_recv).wait()


def add_kernel(blocks, own_ref, cross_ref, out_ref, sums, sems):
    size = own_ref.shape[0] // blocks
    copies = []
    for index in range(blocks):
        span = pl.ds(index * size, size)
        sums[span] = (cross_ref[span] + own_ref[span].astype(jnp.float32)).astype(jnp.bfloat16)
        copies.append(pltpu.make_async_copy(sums.at[span], out_ref.at[span], sems.at[index]))
        copies[-1].start()
    for copy in copies:
        copy.wait()


def fused_body(views, head_parts, *args):
    ray_tokens, up_weight, down_weight, key_weight, value_weight, video_queries = args[:6]
    rows, columns = video_queries.shape
    per_view = columns // HEAD_DIM // views
    ray_rows, ray_width = ray_tokens.shape
    half, inner = up_weight.shape
    share = ray_width // head_parts
    bf16, f32 = jnp.bfloat16, jnp.float32
    dma = pltpu.SemaphoreType.DMA
    anywhere = pl.BlockSpec(memory_space=pl.ANY)
    args = [pltpu.with_memory_space_constraint(arg, pltpu.HBM) for arg in args]
    own, cross = pl.pallas_call(
        functools.partial(kernel, views, head_parts),
        out_shape=(pltpu.VMEM((rows, columns), bf16), pltpu.VMEM((rows, columns), f32)),
        in_specs=[anywhere] * 9,
        out_specs=(anywhere, anywhere),
        scratch_shapes=[
            pltpu.VMEM((2,) + up_weight.shape, bf16),
            pltpu.VMEM((2,) + down_weight.shape, bf16),
            pltpu.VMEM((2 * half, columns), bf16),
            pltpu.VMEM((2 * half, columns), bf16),
            pltpu.VMEM((rows, columns), bf16),
            pltpu.VMEM((ray_rows, ray_width), bf16),
            pltpu.VMEM((ray_rows, inner), bf16),
            pltpu.VMEM((head_parts, ray_rows, share), f32),
            pltpu.VMEM((head_parts, ray_rows, share), f32),
            pltpu.VMEM((2, head_parts, views, ray_rows, share), bf16),
            pltpu.VMEM((per_view, views * rows, HEAD_DIM), bf16),
            pltpu.VMEM((per_view, 2, 2, views * rows, HEAD_DIM), bf16),
            pltpu.VMEM((per_view, views * rows, HEAD_DIM), bf16),
            pltpu.VMEM((rows, HEAD_DIM), bf16),
            pltpu.VMEM((rows, columns), f32),
            dma((6,)),
            dma((4,)),
            dma((4,)),
            dma((per_view,)),
            dma((per_view,)),
            dma((per_view,)),
            dma((3,)),
            dma((per_view,)),
            dma((max(head_parts - 1, 1),)),
            dma((max(head_parts - 1, 1),)),
            dma((views,)),
            dma((views,)),
            dma((max(head_parts - 1, 1),)),
            dma((max(head_parts - 1, 1),)),
            dma,
            dma,
            dma,
            dma,
            dma,
            dma,
            dma((2,)),
            dma,
            pltpu.SemaphoreType.REGULAR((views,)),
            pltpu.SemaphoreType.REGULAR((head_parts,)),
            pltpu.SemaphoreType.REGULAR((2,)),
        ],
        compiler_params=pltpu.CompilerParams(
            collective_id=0, has_side_effects=True, vmem_limit_bytes=48 * 2**20
        ),
    )(*args)
    vmem = pl.BlockSpec(memory_space=pltpu.VMEM)
    blocks = ADD_BLOCKS if rows % (16 * ADD_BLOCKS) == 0 else 1
    return pl.pallas_call(
        functools.partial(add_kernel, blocks),
        out_shape=jax.ShapeDtypeStruct((rows, columns), bf16),
        in_specs=[vmem, vmem],
        out_specs=anywhere,
        scratch_shapes=[pltpu.VMEM((rows, columns), bf16), dma((blocks,))],
        compiler_params=pltpu.CompilerParams(vmem_limit_bytes=8 * 2**20),
    )(
        pltpu.with_memory_space_constraint(own, pltpu.VMEM),
        pltpu.with_memory_space_constraint(cross, pltpu.VMEM),
    )


def solution(mesh):
    views, head_parts = mesh.shape["view"], mesh.shape["head"]

    def routed(*args):
        head_count = args[5].shape[1] // HEAD_DIM
        if (
            mesh.shape["dp"] == 2
            and views % 2 == 0
            and views > 2
            and head_count > views
            and head_count % views == 0
            and args[0].shape[1] % (head_parts * HEAD_DIM) == 0
        ):
            return fused_body(views, head_parts, *args)
        return body(*args)

    in_specs = (
        P(("groups", "view", "dp"), None),
        P("dp", "head"),
        P("dp", "head"),
        P("dp", "head"),
        P("dp", "head"),
        P(("groups", "view", "dp"), "head"),
        P(("groups", "view", "dp"), "head"),
        P(("groups", "view", "dp"), "head"),
        P(("groups", "view", "dp"), "head"),
    )
    out_specs = P(("groups", "view", "dp"), "head")
    return jax.shard_map(routed, mesh=mesh, in_specs=in_specs, out_specs=out_specs, check_vma=False)
```

```python
import functools

import jax
import jax.numpy as jnp
from jax import lax
from jax.experimental import pallas as pl
from jax.experimental.pallas import tpu as pltpu
from jax.sharding import PartitionSpec as P

HEAD_DIM = 128


epsilon = 1e-06


def rms_normed(values_in):
    widened = values_in.astype(jnp.float32)
    mean_square = jnp.mean(widened * widened, axis=1, keepdims=True)
    return widened * lax.rsqrt(mean_square + epsilon)


def empty_state(head_count, row_count):
    running_max = jnp.full((head_count, row_count), -1e30, jnp.float32)
    running_sum = jnp.zeros((head_count, row_count), jnp.float32)
    weighted = jnp.zeros((head_count, row_count, HEAD_DIM), jnp.float32)
    return (running_max, running_sum, weighted)


def absorb(state_now, query_head_rows, key_piece, value_piece):
    running_max, running_sum, weighted = state_now
    head_count = query_head_rows.shape[1]
    key_head_rows = key_piece.reshape(key_piece.shape[0], head_count, HEAD_DIM)
    value_head_rows = value_piece.reshape(value_piece.shape[0], head_count, HEAD_DIM)
    scores = jnp.einsum(
        "xrz,frz->rxf", query_head_rows, key_head_rows, preferred_element_type=jnp.float32
    ) * HEAD_DIM ** (-0.5)
    new_max = jnp.maximum(running_max, jnp.max(scores, axis=2))
    exponent = jnp.exp(scores - new_max[:, :, None])
    running_sum = jnp.sum(exponent, axis=2)
    weighted = jnp.einsum(
        "bau,uby->bay",
        exponent.astype(jnp.bfloat16),
        value_head_rows,
        preferred_element_type=jnp.float32,
    )
    return (new_max, running_sum, weighted)


def finish(state_now):
    running_max, running_sum, weighted = state_now
    result = weighted / running_sum[:, :, None]
    head_count, row_count = running_sum.shape
    return result.transpose(1, 0, 2).reshape(row_count, head_count * HEAD_DIM)


def body(
    ray_tokens,
    up_weight,
    down_weight,
    key_weight,
    value_weight,
    video_queries,
    video_keys,
    video_values,
    cross_queries,
):
    row_count = video_queries.shape[0]
    head_count = video_queries.shape[1] // HEAD_DIM
    up_full, down_full, key_full, value_full = (
        lax.all_gather(up_weight, "dp", axis=0, tiled=True),
        lax.all_gather(down_weight, "dp", axis=0, tiled=True),
        lax.all_gather(key_weight, "dp", axis=0, tiled=True),
        lax.all_gather(value_weight, "dp", axis=0, tiled=True),
    )
    normed = rms_normed(ray_tokens).astype(jnp.bfloat16)
    hidden = jax.nn.gelu(jnp.dot(normed, up_full, preferred_element_type=jnp.float32)).astype(
        jnp.bfloat16
    )
    partial_branch = lax.dot_general(
        hidden, down_full, (((1,), (1,)), ((), ())), preferred_element_type=jnp.float32
    )
    branch = lax.psum(partial_branch, "head")
    rays = (ray_tokens.astype(jnp.float32) + branch).astype(jnp.bfloat16)
    cross_heads = cross_queries.reshape(row_count, head_count, HEAD_DIM)
    piece = lax.all_gather(rays, ("view", "dp"), axis=0, tiled=True)
    piece_keys = jnp.dot(piece, key_full, preferred_element_type=jnp.float32).astype(jnp.bfloat16)
    piece_values = jnp.dot(piece, value_full, preferred_element_type=jnp.float32).astype(
        jnp.bfloat16
    )
    cross_state = absorb(empty_state(head_count, row_count), cross_heads, piece_keys, piece_values)
    cross = finish(cross_state)
    local_head_group = video_queries.reshape(row_count, head_count, HEAD_DIM)
    own_state = absorb(
        empty_state(head_count, row_count),
        local_head_group,
        lax.all_gather(video_keys, ("view", "dp"), axis=0, tiled=True),
        lax.all_gather(video_values, ("view", "dp"), axis=0, tiled=True),
    )
    own = finish(own_state)
    return (own + cross).astype(jnp.bfloat16)


MESH = pl.DeviceIdType.MESH
QUERY_BLOCK = 256
FIRST_HEADS = 2
SECOND_HEADS = 1
NOT_DEFERRED = 1
SENT_AHEAD = 2
ADD_BLOCKS = 8


def softmax_mix(queries, keys, values):
    scores = lax.dot_general(
        queries, keys, (((1,), (1,)), ((), ())), preferred_element_type=jnp.float32
    )
    largest = jnp.max(scores, axis=1, keepdims=True)
    weights = jnp.exp((scores - largest) * HEAD_DIM ** (-0.5))
    row_sums = jnp.sum(weights, axis=1, keepdims=True)
    mixed = jnp.dot(weights.astype(jnp.bfloat16), values, preferred_element_type=jnp.float32)
    return mixed / row_sums


def columns_of(index):
    return pl.ds(pl.multiple_of(index * HEAD_DIM, HEAD_DIM), HEAD_DIM)


def kernel(
    views,
    head_parts,
    ray_ref,
    up_ref,
    down_ref,
    key_ref,
    value_ref,
    query_ref,
    video_key_ref,
    video_value_ref,
    cross_query_ref,
    own_ref,
    cross_out_ref,
    up_full,
    down_full,
    key_full,
    value_full,
    cross_queries,
    ray_tokens,
    hidden_ref,
    partials_out,
    partials_in,
    rays,
    query_heads,
    pair_heads,
    own_heads,
    detour_ref,
    cross_ref,
    weight_local,
    weight_send,
    weight_recv,
    query_recv,
    pair_recv,
    relay_recv,
    bulk_send,
    relay_send,
    partial_send,
    partial_recv,
    ray_send,
    ray_recv,
    share_send,
    share_recv,
    pair_ray_send,
    pair_ray_recv,
    own_send,
    own_recv,
    own_local,
    cross_sem,
    detour_send,
    detour_recv,
    view_greeted,
    part_greeted,
    core_greeted,
):
    view = lax.axis_index("view")
    part = lax.axis_index("head")
    core = lax.axis_index("dp")
    other = 1 - core
    rows = query_ref.shape[0]
    head_count = query_ref.shape[1] // HEAD_DIM
    per_view = head_count // views
    ray_rows = ray_ref.shape[0]
    half = up_ref.shape[0]
    inner = up_ref.shape[1]
    share = ray_ref.shape[1] // head_parts
    side = views // 2

    peers = [lax.rem(view + step, views) for step in range(1, views)]
    part_peers = [lax.rem(part + step, head_parts) for step in range(1, head_parts)]

    ordered_peers = [jnp.where(step < view, view - 1 - step, step + 1) for step in range(views - 1)]

    barrier = pltpu.get_barrier_semaphore()

    def enter(axis, peer, first):
        @pl.when(first)
        def _():
            pl.semaphore_signal(barrier, inc=1, device_id={axis: peer}, device_id_type=MESH)

    def answer(axis, peer, position, greeted, second):
        @pl.when(second)
        def _():
            pl.semaphore_signal(
                greeted.at[position], inc=1, device_id={axis: peer}, device_id_type=MESH
            )

    for peer in part_peers:
        enter("head", peer, part < peer)
    enter("dp", other, core == 1)
    for peer in ordered_peers:
        enter("view", peer, view < peer)
    earlier = view + part + other

    @pl.when(earlier > 0)
    def _():
        pl.semaphore_wait(barrier, earlier)

    for peer in ordered_peers:
        answer("view", peer, view, view_greeted, view > peer)
    for peer in part_peers:
        answer("head", peer, part, part_greeted, part > peer)
    answer("dp", other, core, core_greeted, core == 0)

    depth = pl.ds(pl.multiple_of(core * half, half), half)
    weight_pairs = (
        (up_ref, up_full.at[core]),
        (down_ref, down_full.at[core]),
        (key_ref, key_full.at[depth]),
        (value_ref, value_full.at[depth]),
    )
    local_copies = [
        pltpu.make_async_copy(source, slot, weight_local.at[index])
        for index, (source, slot) in enumerate(weight_pairs)
    ]
    local_copies.append(
        pltpu.make_async_copy(cross_query_ref, cross_queries, weight_local.at[4])
    )
    remote_copies = [
        pltpu.make_async_remote_copy(
            src_ref=source,
            dst_ref=slot,
            send_sem=weight_send.at[index],
            recv_sem=weight_recv.at[index],
            device_id={"dp": other},
            device_id_type=MESH,
        )
        for index, (source, slot) in enumerate(weight_pairs)
    ]
    local_copies.append(pltpu.make_async_copy(ray_ref, ray_tokens, weight_local.at[5]))
    own_rows = pl.ds(pl.multiple_of(view * rows, rows), rows)

    def keep_heads(index, carry):
        columns = columns_of(view * per_view + index)
        pltpu.make_async_copy(
            query_ref.at[:, columns], query_heads.at[index, own_rows], query_recv.at[index]
        ).start()
        pltpu.make_async_copy(
            video_key_ref.at[:, columns],
            pair_heads.at[index, core, 0, own_rows],
            pair_recv.at[index],
        ).start()
        pltpu.make_async_copy(
            video_value_ref.at[:, columns],
            pair_heads.at[index, core, 1, own_rows],
            pair_recv.at[index],
        ).start()
        return carry


    def send_head(index, peer):
        columns = columns_of(peer * per_view + index)
        for tensor, (source, target, arrived) in enumerate((
            (video_key_ref, pair_heads.at[index, core, 0, own_rows], pair_recv.at[index]),
            (video_value_ref, pair_heads.at[index, core, 1, own_rows], pair_recv.at[index]),
            (query_ref, query_heads.at[index, own_rows], query_recv.at[index]),
        )):
            pltpu.make_async_remote_copy(
                src_ref=source.at[:, columns],
                dst_ref=target,
                send_sem=bulk_send.at[tensor],
                recv_sem=arrived,
                device_id={"view": peer},
                device_id_type=MESH,
            ).start()

    def send_heads(index, carry):
        for peer in peers:
            send_head(index, peer)
        return carry

    def send_far(index, carry):
        for peer in peers:
            @pl.when(peer // side != view // side)
            def _():
                send_head(index, peer)
        return carry

    def send_near(index, carry):
        for peer in peers:
            @pl.when(peer // side == view // side)
            def _():
                send_head(index, peer)
        return carry

    first_heads = min(FIRST_HEADS, per_view)
    for step, peer in enumerate(ordered_peers):
        @pl.when(step >= view)
        def _():
            pl.semaphore_wait(view_greeted.at[step + 1], 1)

        def send_first(index, carry):
            send_head(index, peer)
            return carry

        lax.fori_loop(0, first_heads, send_first, 0)

    @pl.when(core == 1)
    def _():
        pl.semaphore_wait(core_greeted.at[0], 1)

    for copy in remote_copies[:2]:
        copy.start()
    for copy in local_copies[::-1]:
        copy.start()
    lax.fori_loop(0, per_view, keep_heads, 0)
    for copy in remote_copies[2:]:
        copy.start()

    local_copies[5].wait()
    tokens = ray_tokens[...]
    normed = rms_normed(tokens).astype(jnp.bfloat16)
    local_copies[0].wait()
    remote_copies[0].wait_recv()
    tile = min(512, inner)

    def up_tile(index, carry):
        columns = pl.ds(pl.multiple_of(index * tile, tile), tile)
        total = jnp.dot(normed[:, :half], up_full[0, :, columns], preferred_element_type=jnp.float32)
        total += jnp.dot(normed[:, half:], up_full[1, :, columns], preferred_element_type=jnp.float32)
        hidden_ref[:, columns] = jax.nn.gelu(total).astype(jnp.bfloat16)
        return carry

    lax.fori_loop(0, inner // tile, up_tile, 0)
    local_copies[1].wait()
    remote_copies[1].wait_recv()
    branch = jnp.concatenate(
        [
            lax.dot_general(
                hidden_ref[...],
                down_full[index],
                (((1,), (1,)), ((), ())),
                preferred_element_type=jnp.float32,
            )
            for index in range(2)
        ],
        axis=1,
    )
    for index in range(head_parts):
        partials_out[index] = branch[:, index * share : (index + 1) * share]
    partial_copies = [
        pltpu.make_async_remote_copy(
            src_ref=partials_out.at[peer],
            dst_ref=partials_in.at[step],
            send_sem=partial_send.at[step],
            recv_sem=partial_recv.at[step],
            device_id={"head": peer},
            device_id_type=MESH,
        )
        for step, peer in enumerate(part_peers)
    ]
    for later in range(1, head_parts):
        @pl.when(part < later)
        def _():
            pl.semaphore_wait(part_greeted.at[later], 1)

    for copy in partial_copies:
        copy.start()
    for copy in partial_copies:
        copy.wait_recv()
    total_share = partials_out[part]
    for index in range(head_parts - 1):
        total_share += partials_in[index]
    share_columns = pl.ds(pl.multiple_of(part * share, share), share)
    rays[core, part, view] = (
        ray_tokens[:, share_columns].astype(jnp.float32) + total_share
    ).astype(jnp.bfloat16)
    side_start = (view // side) * side
    far_start = side - side_start
    gate = jnp.where(side_start == 0, side - 1, side)
    far_gate = 2 * side - 1 - gate
    side_peers = [side_start + lax.rem(view - side_start + step, side) for step in range(1, side)]

    def ray_copy(source, peer, index, arrived):
        return pltpu.make_async_remote_copy(
            src_ref=source,
            dst_ref=source,
            send_sem=ray_send.at[index],
            recv_sem=ray_recv.at[arrived],
            device_id={"view": peer},
            device_id_type=MESH,
        )

    mine = rays.at[core, part, view]
    far_slots = rays.at[core, part, pl.ds(far_start, side)]
    ray_copies = [ray_copy(mine, peer, step, step) for step, peer in enumerate(side_peers)]
    far_copy = ray_copy(mine, far_gate, side - 1, side - 1)
    far_copy.start()
    for copy in ray_copies:
        copy.start()
    second_heads = min(first_heads + SECOND_HEADS, per_view)
    facing_view = jnp.logical_or(view == side - 1, view == side)

    @pl.when(facing_view)
    def _():
        lax.fori_loop(first_heads, second_heads, send_heads, 0)
        lax.fori_loop(second_heads, per_view, send_far, 0)


    def relay(index):
        return pltpu.make_async_remote_copy(
            src_ref=pair_heads.at[index, core],
            dst_ref=pair_heads.at[index, core],
            send_sem=relay_send.at[index],
            recv_sem=relay_recv.at[index],
            device_id={"dp": other},
            device_id_type=MESH,
        )

    def pass_on(index, carry):
        arrived = pair_heads.at[index, core]
        pltpu.make_async_copy(arrived, arrived, pair_recv.at[index]).wait()
        relay(index).start()
        return carry

    last_view = far_start + side - 1

    def own_copy(index, peer):
        return pltpu.make_async_remote_copy(
            src_ref=own_heads.at[index, pl.ds(pl.multiple_of(peer * rows, rows), rows)],
            dst_ref=own_ref.at[:, columns_of(view * per_view + index)],
            send_sem=own_send,
            recv_sem=own_recv,
            device_id={"view": peer},
            device_id_type=MESH,
        )

    gives = core == 0
    takes = core == 1
    detour_in = pltpu.make_async_remote_copy(
        src_ref=own_heads.at[per_view - 1, pl.ds(pl.multiple_of(last_view * rows, rows), rows)],
        dst_ref=detour_ref,
        send_sem=detour_send.at[0],
        recv_sem=detour_recv,
        device_id={"dp": other},
        device_id_type=MESH,
    )
    detour_out = pltpu.make_async_remote_copy(
        src_ref=detour_ref,
        dst_ref=own_ref.at[:, columns_of(view * per_view + per_view - 1)],
        send_sem=detour_send.at[1],
        recv_sem=own_recv,
        device_id={"view": last_view, "dp": other},
        device_id_type=MESH,
    )

    def send_last(index, carry):
        own_copy(index, last_view).start()
        return carry

    holds = jnp.logical_not(facing_view)

    def not_last(index, peer):
        return jnp.logical_or(index < NOT_DEFERRED, peer != last_view)

    def attend(index, carry):
        arrived = query_heads.at[index]
        pltpu.make_async_copy(arrived, arrived, query_recv.at[index]).wait()
        relay(index).wait_recv()
        keys = pair_heads[index, :, 0].reshape(2 * views * rows, HEAD_DIM)
        values = pair_heads[index, :, 1].reshape(2 * views * rows, HEAD_DIM)
        block = min(QUERY_BLOCK, views * rows)

        def attend_block(piece, inner_carry):
            span = pl.ds(pl.multiple_of(piece * block, block), block)
            own_heads[index, span] = softmax_mix(query_heads[index, span], keys, values).astype(
                jnp.bfloat16
            )
            return inner_carry

        lax.fori_loop(0, views * rows // block, attend_block, 0)
        columns = columns_of(view * per_view + index)
        pltpu.make_async_copy(
            own_heads.at[index, own_rows], own_ref.at[:, columns], own_local
        ).start()
        for peer in peers:
            held = jnp.logical_and(
                jnp.logical_and(holds, index < second_heads), peer // side != view // side
            )

            @pl.when(jnp.logical_and(not_last(index, peer), jnp.logical_not(held)))
            def _():
                own_copy(index, peer).start()

        return carry

    def send_held(index, carry):
        for peer in peers:
            far = peer // side != view // side

            @pl.when(jnp.logical_and(not_last(index, peer), far))
            def _():
                own_copy(index, peer).start()

        return carry

    lax.fori_loop(0, 1, pass_on, 0)

    @pl.when(jnp.logical_not(facing_view))
    def _():
        lax.fori_loop(first_heads, second_heads, send_heads, 0)

    lax.fori_loop(1, first_heads, pass_on, 0)
    pltpu.make_async_copy(far_slots, far_slots, ray_recv.at[side - 1]).wait()
    gate_copies = [
        ray_copy(far_slots, peer, side + step, side - 1) for step, peer in enumerate(side_peers)
    ]

    @pl.when(view == gate)
    def _():
        for copy in gate_copies:
            copy.start()


    @pl.when(facing_view)
    def _():
        lax.fori_loop(second_heads, per_view, send_near, 0)
        lax.fori_loop(per_view, per_view, send_heads, 0)

    @pl.when(jnp.logical_not(facing_view))
    def _():
        lax.fori_loop(second_heads, per_view, send_heads, 0)

    for copy in ray_copies:
        copy.wait_recv()
    share_copies = [
        pltpu.make_async_remote_copy(
            src_ref=rays.at[core, part],
            dst_ref=rays.at[core, part],
            send_sem=share_send.at[step],
            recv_sem=share_recv.at[step],
            device_id={"head": peer},
            device_id_type=MESH,
        )
        for step, peer in enumerate(part_peers)
    ]
    for copy in share_copies:
        copy.start()
    lax.fori_loop(0, first_heads, attend, 0)
    lax.fori_loop(first_heads, second_heads, pass_on, 0)
    for copy in share_copies:
        copy.wait_recv()
    ray_relay = pltpu.make_async_remote_copy(
        src_ref=rays.at[core],
        dst_ref=rays.at[core],
        send_sem=pair_ray_send,
        recv_sem=pair_ray_recv,
        device_id={"dp": other},
        device_id_type=MESH,
    )
    ray_relay.start()
    lax.fori_loop(first_heads, second_heads, attend, 0)

    ray_relay.wait_recv()
    for index in (2, 3):
        local_copies[index].wait()
        remote_copies[index].wait_recv()
    local_copies[4].wait()
    ray_shares = [
        rays[:, index].reshape(2 * views * ray_rows, share) for index in range(head_parts)
    ]
    group = 2 if head_count % 2 == 0 else 1
    width = group * HEAD_DIM

    def cross_group(index, carry):
        columns = pl.ds(pl.multiple_of(index * width, width), width)

        def project(full):
            total = 0.0
            for index, ray_share in enumerate(ray_shares):
                total += jnp.dot(
                    ray_share,
                    full[index * share : (index + 1) * share, columns],
                    preferred_element_type=jnp.float32,
                )
            return total.astype(jnp.bfloat16)

        keys, values = project(key_full), project(value_full)
        queries = cross_queries[:, columns]
        results = []
        for lane in range(group):
            span = slice(lane * HEAD_DIM, (lane + 1) * HEAD_DIM)
            results.append(softmax_mix(queries[:, span], keys[:, span], values[:, span]))
        cross_ref[:, columns] = jnp.concatenate(results, axis=1)
        return carry

    lax.fori_loop(0, head_count // group, cross_group, 0)
    cross_copy = pltpu.make_async_copy(cross_ref, cross_out_ref, cross_sem)
    cross_copy.start()

    lax.fori_loop(second_heads, per_view, pass_on, 0)

    @pl.when(holds)
    def _():
        lax.fori_loop(0, second_heads, send_held, 0)

    last_head = max(second_heads, per_view - 1)
    sent_ahead = jnp.logical_and(jnp.logical_and(holds, view >= side), core == 1)
    middle = jnp.where(sent_ahead, min(SENT_AHEAD, per_view), NOT_DEFERRED)
    lax.fori_loop(second_heads, last_head, attend, 0)
    lax.fori_loop(NOT_DEFERRED, middle, send_last, 0)
    lax.fori_loop(last_head, per_view, attend, 0)

    @pl.when(gives)
    def _():
        detour_in.start()

    @pl.when(takes)
    def _():
        detour_in.wait_recv()
        detour_out.start()

    lax.fori_loop(middle, jnp.where(gives, per_view - 1, per_view), send_last, 0)

    sent_copies = remote_copies + partial_copies + ray_copies + share_copies
    for copy in sent_copies + [far_copy, ray_relay]:
        copy.wait_send()

    @pl.when(view == gate)
    def _():
        for copy in gate_copies:
            copy.wait_send()

    def relay_sent(index, carry):
        relay(index).wait_send()
        return carry

    lax.fori_loop(0, per_view, relay_sent, 0)
    for tensor in range(3):
        sent = query_heads.at[:, pl.ds(0, (views - 1) * rows)]
        pltpu.make_async_copy(sent, sent, bulk_send.at[tensor]).wait()
    cross_copy.wait()
    kept = own_heads.at[:, pl.ds(0, rows)]
    pltpu.make_async_copy(kept, kept, own_local).wait()
    returned = own_heads.at[:, pl.ds(0, (views - 1) * rows)]
    direct = own_heads.at[pl.ds(0, per_view - 1), pl.ds(0, (views - 1) * rows)]
    pltpu.make_async_copy(direct, direct, own_send).wait()
    direct = own_heads.at[0, pl.ds(0, (views - 2) * rows)]
    pltpu.make_async_copy(direct, direct, own_send).wait()

    @pl.when(gives)
    def _():
        detour_in.wait_send()

    @pl.when(jnp.logical_not(gives))
    def _():
        single = own_heads.at[0, pl.ds(0, rows)]
        pltpu.make_async_copy(single, single, own_send).wait()

    @pl.when(takes)
    def _():
        detour_out.wait_send()

    pltpu.make_async_copy(returned, returned, own_recv).wait()


def add_kernel(blocks, own_ref, cross_ref, out_ref, sums, sems):
    size = own_ref.shape[0] // blocks
    copies = []
    for index in range(blocks):
        span = pl.ds(index * size, size)
        sums[span] = (cross_ref[span] + own_ref[span].astype(jnp.float32)).astype(jnp.bfloat16)
        copies.append(pltpu.make_async_copy(sums.at[span], out_ref.at[span], sems.at[index]))
        copies[-1].start()
    for copy in copies:
        copy.wait()


def fused_body(views, head_parts, *args):
    ray_tokens, up_weight, down_weight, key_weight, value_weight, video_queries = args[:6]
    rows, columns = video_queries.shape
    per_view = columns // HEAD_DIM // views
    ray_rows, ray_width = ray_tokens.shape
    half, inner = up_weight.shape
    share = ray_width // head_parts
    bf16, f32 = jnp.bfloat16, jnp.float32
    dma = pltpu.SemaphoreType.DMA
    anywhere = pl.BlockSpec(memory_space=pl.ANY)
    args = [pltpu.with_memory_space_constraint(arg, pltpu.HBM) for arg in args]
    own, cross = pl.pallas_call(
        functools.partial(kernel, views, head_parts),
        out_shape=(pltpu.VMEM((rows, columns), bf16), pltpu.VMEM((rows, columns), f32)),
        in_specs=[anywhere] * 9,
        out_specs=(anywhere, anywhere),
        scratch_shapes=[
            pltpu.VMEM((2,) + up_weight.shape, bf16),
            pltpu.VMEM((2,) + down_weight.shape, bf16),
            pltpu.VMEM((2 * half, columns), bf16),
            pltpu.VMEM((2 * half, columns), bf16),
            pltpu.VMEM((rows, columns), bf16),
            pltpu.VMEM((ray_rows, ray_width), bf16),
            pltpu.VMEM((ray_rows, inner), bf16),
            pltpu.VMEM((head_parts, ray_rows, share), f32),
            pltpu.VMEM((head_parts, ray_rows, share), f32),
            pltpu.VMEM((2, head_parts, views, ray_rows, share), bf16),
            pltpu.VMEM((per_view, views * rows, HEAD_DIM), bf16),
            pltpu.VMEM((per_view, 2, 2, views * rows, HEAD_DIM), bf16),
            pltpu.VMEM((per_view, views * rows, HEAD_DIM), bf16),
            pltpu.VMEM((rows, HEAD_DIM), bf16),
            pltpu.VMEM((rows, columns), f32),
            dma((6,)),
            dma((4,)),
            dma((4,)),
            dma((per_view,)),
            dma((per_view,)),
            dma((per_view,)),
            dma((3,)),
            dma((per_view,)),
            dma((max(head_parts - 1, 1),)),
            dma((max(head_parts - 1, 1),)),
            dma((views,)),
            dma((views,)),
            dma((max(head_parts - 1, 1),)),
            dma((max(head_parts - 1, 1),)),
            dma,
            dma,
            dma,
            dma,
            dma,
            dma,
            dma((2,)),
            dma,
            pltpu.SemaphoreType.REGULAR((views,)),
            pltpu.SemaphoreType.REGULAR((head_parts,)),
            pltpu.SemaphoreType.REGULAR((2,)),
        ],
        compiler_params=pltpu.CompilerParams(
            collective_id=0, has_side_effects=True, vmem_limit_bytes=48 * 2**20
        ),
    )(*args)
    vmem = pl.BlockSpec(memory_space=pltpu.VMEM)
    blocks = ADD_BLOCKS if rows % (16 * ADD_BLOCKS) == 0 else 1
    return pl.pallas_call(
        functools.partial(add_kernel, blocks),
        out_shape=jax.ShapeDtypeStruct((rows, columns), bf16),
        in_specs=[vmem, vmem],
        out_specs=anywhere,
        scratch_shapes=[pltpu.VMEM((rows, columns), bf16), dma((blocks,))],
        compiler_params=pltpu.CompilerParams(vmem_limit_bytes=8 * 2**20),
    )(
        pltpu.with_memory_space_constraint(own, pltpu.VMEM),
        pltpu.with_memory_space_constraint(cross, pltpu.VMEM),
    )


def solution(mesh):
    views, head_parts = mesh.shape["view"], mesh.shape["head"]

    def routed(*args):
        head_count = args[5].shape[1] // HEAD_DIM
        if (
            mesh.shape["dp"] == 2
            and views % 2 == 0
            and views > 2
            and head_count > views
            and head_count % views == 0
            and args[0].shape[1] % (head_parts * HEAD_DIM) == 0
        ):
            return fused_body(views, head_parts, *args)
        return body(*args)

    in_specs = (
        P(("groups", "view", "dp"), None),
        P("dp", "head"),
        P("dp", "head"),
        P("dp", "head"),
        P("dp", "head"),
        P(("groups", "view", "dp"), "head"),
        P(("groups", "view", "dp"), "head"),
        P(("groups", "view", "dp"), "head"),
        P(("groups", "view", "dp"), "head"),
    )
    out_specs = P(("groups", "view", "dp"), "head")
    return jax.shard_map(routed, mesh=mesh, in_specs=in_specs, out_specs=out_specs, check_vma=False)
```
